32 devices in a mesh: grp: 4 (over y, x), dev: 8 (over z, core).
Axes of the slice: x: 2, y: 2, z: 4, core: 2. Of those that a mesh axis runs over, the one named last changes fastest.
Arguments:
- tiles: bfloat16 [128, 9, 4, 4, 128], P(('grp', 'dev')), may hold values from -6 to 6
- cotangent: bfloat16 [128, 9, 8, 8, 128], P(('grp', 'dev')), may hold values from -6 to 6
- weight: bfloat16 [3456, 128], P('dev'), may hold values from -0.109375 to 0.109375
- bias: float32 [128], replicated, may hold values from -4 to 4
- counts: int32 [32], replicated, may hold values from 1 to 4, as said below
Outputs:
- grad_weight: float32 [3456, 128], P('dev')
- grad_bias: float32 [128], P('dev')
The draws below stay inside these ranges and needn't reach their ends.
Inputs may be any that keep to these rules, and one draw needn't show every extreme that they name: `counts`: every group of 8 devices has at least one device with 4 live tiles; live tiles fill the first slots of a device.
All inputs are finite; a program needn't handle non-finite values.
Results may differ from the reference program's by a relative error of at most 0.0049.
Values may be sent and summed in bfloat16 or wider, within the bound.
A program may use at most 64 MiB of HBM per device.

```python
import jax
import jax.numpy as jnp
from jax import lax

CIN = 128
COUT = 128
F = 9
HL = 4
WL = 4
CAP = 4
SLOTS = 128
N_GRP = 4
N_DEV = 8


def draw_counts(key, part):
    total = N_GRP * N_DEV
    first, second = jax.random.split(jax.random.fold_in(key, 17))
    heavy = jax.random.randint(first, (total,), 0, 5) == 0
    base = jnp.where(heavy, CAP, 1).astype(jnp.int32).reshape(N_GRP, N_DEV)
    chosen = jax.random.randint(second, (N_GRP,), 0, N_DEV)
    forced = jnp.arange(N_DEV)[None, :] == chosen[:, None]
    return jnp.where(forced, CAP, base).astype(jnp.int32).reshape(total)


def spiked(array, key, source, target, shards_of, factor):
    owner, partner = [(jnp.arange(array.shape[dim]) // (array.shape[dim] // shards_of)).reshape([-1 if axis == dim else 1 for axis in range(array.ndim)]) for dim in (source, target)]
    chosen = jax.random.permutation(key, shards_of)[partner]
    strong = (owner == chosen) | (owner == (partner + shards_of // 2) % shards_of)
    return jnp.where(strong, factor * array, array)


def block_levels(stream_key, shape, shards, least, largest):
    gain = 1.0
    for dim, shards_of in shards:
        draws = jax.random.uniform(jax.random.fold_in(jax.random.fold_in(stream_key, 6), dim), (shards_of,), jnp.float32, least / len(shards), largest / len(shards))
        gain = gain * jnp.repeat(jnp.exp(draws), shape[dim] // shards_of).reshape((-1,) + (1,) * (len(shape) - 1 - dim))
    return gain


def scatter_about(stream_key, dims, scale, limit, cuts=(), kind=jnp.bfloat16):
    entries = jax.random.normal(stream_key, dims, jnp.float32) * scale
    if len(cuts) > 0:
        entries = block_levels(stream_key, dims, cuts, -0.22, 0.18) * entries
    return jnp.clip(entries, min=-limit, max=limit).astype(kind)


def bell_draw_with(key, dims, scale, reach, shards, heavy, kind=jnp.bfloat16):
    values = scale * jax.random.normal(key, dims, jnp.float32)
    if shards:
        values = values * block_levels(key, dims, shards, -0.22, 0.18)
    return jnp.clip(spiked(values, jax.random.fold_in(key, 3), *heavy), -reach, reach).astype(kind)


def setup_inputs(seed: int = 0) -> dict:
    keys = jax.random.split(jax.random.key(seed), 6)
    return {
        "tiles": bell_draw_with(keys[0], (SLOTS, F, HL, WL, CIN), 1.0, 6.0, ((0, 32),), (0, 4, 32, 2.75)),
        "cotangent": scatter_about(keys[1], (SLOTS, F, 2 * HL, 2 * WL, COUT), 1.0, 6.0, ((0, 32),)),
        "weight": scatter_about(keys[2], (27 * CIN, COUT), (27 * CIN) ** -0.5, 0.109375, ((0, 8),)),
        "bias": scatter_about(keys[3], (COUT,), 1.0, 4.0, (), jnp.float32),
        "counts": draw_counts(jax.random.fold_in(keys[5], 71), 0),
    }


def padded_input(tile):
    up = jnp.repeat(jnp.repeat(tile, 2, axis=1), 2, axis=2)
    up = jnp.concatenate([up[:1], up[:1], up], axis=0)
    return jnp.pad(up, ((0, 0), (1, 1), (1, 1), (0, 0)))

def window_list(padded, frames, height, width):
    chans = padded.shape[-1]
    result = []
    for kd in range(3):
        for kh in range(3):
            for kw in range(3):
                piece = padded[kd:kd + frames, kh:kh + height, kw:kw + width, :]
                result.append(piece.reshape(frames * height * width, chans))
    return result

def tile_terms(tile, cot, taps, bias):
    frames, height, width = (tile.shape[0], 2 * tile.shape[1], 2 * tile.shape[2])
    windows = window_list(padded_input(tile), frames, height, width)
    z = jnp.zeros((frames * height * width, taps.shape[2]), jnp.float32) + bias.astype(jnp.float32)
    for k in range(27):
        z = z + jnp.dot(windows[k], taps[k], preferred_element_type=jnp.float32)
    sig = jax.nn.sigmoid(z)
    dz = (cot.reshape(z.shape).astype(jnp.float32) * sig * (1.0 + z * (1.0 - sig))).astype(jnp.bfloat16)
    grads = [lax.dot_general(windows[k], dz, (((0,), (0,)), ((), ())), preferred_element_type=jnp.float32) for k in range(27)]
    return (jnp.stack(grads, 0), lax.optimization_barrier(jnp.sum(dz.astype(jnp.float32), axis=0)))

def reference(tiles, cotangent, weight, bias, counts):
    cin = tiles.shape[-1]
    cout = weight.shape[1]
    taps = weight.reshape(cin, 27, cout).transpose(1, 0, 2)
    slots = tiles.shape[0]
    cap = slots // counts.shape[0]
    cells = tiles.shape[1] * 4 * tiles.shape[2] * tiles.shape[3]
    scale = 1.0 / jnp.sqrt(jnp.float32(slots * cells))

    def step(carry, index):
        live = index % cap < counts[index // cap]

        def compute(args):
            return tile_terms(tiles[index], cotangent[index], taps, bias)

        def skip(args):
            return (jnp.zeros((27, cin, cout), jnp.float32), jnp.zeros((cout,), jnp.float32))
        gw, gb = lax.cond(live, compute, skip, 0)
        return ((carry[0] + gw, carry[1] + gb), None)
    init = (jnp.zeros((27, cin, cout), jnp.float32), jnp.zeros((cout,), jnp.float32))
    (gw, gb), _ = lax.scan(step, init, jnp.arange(slots, dtype=jnp.int32))
    grad_weight = gw.transpose(1, 0, 2).reshape(cin * 27, cout) * scale
    return (grad_weight, gb * scale)
```

```python
import functools
import math

import jax
import jax.numpy as jnp
from jax import lax
from jax.experimental import pallas as pl
from jax.experimental.pallas import tpu as pltpu
from jax.sharding import PartitionSpec as P

MESH = pl.DeviceIdType.MESH
TAPS = {(0, 0): (0,), (0, 1): (1, 2), (1, 0): (0, 1), (1, 1): (2,)}
OFFSET = ((0, 1, 1), (0, 0, 1))


def build_windows(x_ref, f_ref, xs_ref):
    rows = x_ref.shape[0]
    slab = rows // 4
    pad = 40
    row = lax.broadcasted_iota(jnp.int32, (rows, 128), 0).astype(jnp.float32)
    frame = row - 9.0 * jnp.floor((row + 0.5) * (1.0 / 9.0))
    place = lax.broadcasted_iota(jnp.int32, (slab, 128), 0)
    xs_ref[0:slab] = jnp.zeros((slab, 1152), jnp.bfloat16)
    xs_ref[5 * slab : 6 * slab] = jnp.zeros((slab, 1152), jnp.bfloat16)
    f_ref[...] = jnp.zeros_like(f_ref)
    now = x_ref[...].astype(jnp.float32)
    f_ref[2, pad : pad + rows] = now
    back1 = jnp.where(frame < 0.5, now, f_ref[2, pad - 1 : pad - 1 + rows])
    f_ref[1, pad : pad + rows] = back1
    f_ref[0, pad : pad + rows] = jnp.where(
        frame < 1.5, back1, f_ref[2, pad - 2 : pad - 2 + rows]
    )
    for h in range(4):
        for dw in range(3):
            for kd in range(3):
                start = pad + h * slab + (dw - 1) * 36
                piece = f_ref[kd, start : start + slab]
                if dw == 0:
                    piece = jnp.where(place < 36, 0.0, piece)
                if dw == 2:
                    piece = jnp.where(place >= slab - 36, 0.0, piece)
                col = dw * 384 + kd * 128
                xs_ref[(h + 1) * slab : (h + 2) * slab, col : col + 128] = piece.astype(
                    jnp.bfloat16
                )


def combine_weights(w_ref, wz_ref):
    chans = 128
    for kd in range(3):
        tap = {}
        for kh in range(3):
            for kw in range(3):
                piece = w_ref[:, 9 * kd + 3 * kh + kw]
                tap[kh, kw] = piece.reshape(chans, chans).astype(jnp.float32)
        for ph in range(2):
            for a in range(2):
                line = [sum(tap[kh, kw] for kh in TAPS[ph, a]) for kw in range(3)]
                for pw in range(2):
                    for b in range(2):
                        both = sum(line[kw] for kw in TAPS[pw, b])
                        row = (b + pw) * 384 + kd * 128
                        col = (2 * ph + pw) * 128
                        wz_ref[a + ph, row : row + 128, col : col + 128] = both.astype(
                            jnp.bfloat16
                        )


def products(count, xs_ref, cot_ref, bias_ref, wz_ref, g_ref):
    slab = xs_ref.shape[0] // 6
    rows = 4 * slab
    row = lax.broadcasted_iota(jnp.int32, (rows, 128), 0).astype(jnp.float32)
    place = row - 36.0 * jnp.floor((row + 0.5) * (1.0 / 36.0))
    live = place < 9.0 * count.astype(jnp.float32)
    cols = ((0, 256), (0, 512), (256, 256))

    def window(dh):
        return xs_ref[dh * slab : dh * slab + rows, :]

    mid = jnp.dot(window(1), wz_ref[1], preferred_element_type=jnp.float32)
    top = jnp.dot(window(0), wz_ref[0, :, 0:256], preferred_element_type=jnp.float32)
    low = jnp.dot(window(2), wz_ref[2, :, 256:512], preferred_element_type=jnp.float32)
    parts = []
    total_b = jnp.zeros((1, 128), jnp.float32)
    for p in range(4):
        side = (top if p < 2 else low)[:, (p % 2) * 128 : (p % 2) * 128 + 128]
        z = mid[:, p * 128 : p * 128 + 128] + side + bias_ref[...]
        sig = jax.nn.sigmoid(z)
        dz = cot_ref[p].astype(jnp.float32) * sig * (1.0 + z * (1.0 - sig))
        dz = jnp.where(live, dz, 0.0).astype(jnp.bfloat16)
        total_b += jnp.sum(dz.astype(jnp.float32), axis=0, keepdims=True)
        parts.append(dz)
    dz = jnp.concatenate(parts, axis=1)
    for dh in range(3):
        start, width = cols[dh]
        g_ref[dh, :, start : start + width] = lax.dot_general(
            window(dh),
            dz[:, start : start + width],
            (((0,), (0,)), ((), ())),
            preferred_element_type=jnp.float32,
        )
    return total_b


def tap_gradient(g_ref, k, base=0, size=128):
    kd, kh, kw = k // 9, k // 3 % 3, k % 3
    total = None
    for ph in range(2):
        for pw in range(2):
            row = (OFFSET[pw][kw] + pw) * 384 + kd * 128
            col = (2 * ph + pw) * 128
            term = g_ref[
                OFFSET[ph][kh] + ph, pl.ds(base + row, size), col : col + 128
            ]
            total = term if total is None else total + term
    return total


WORK = [
    pltpu.VMEM((3, 656, 128), jnp.float32),
    pltpu.VMEM((864, 1152), jnp.bfloat16),
    pltpu.VMEM((3, 1152, 512), jnp.bfloat16),
    pltpu.VMEM((3, 1152, 512), jnp.float32),
]


def terms_kernel(
    count_ref, w_ref, x_ref, cot_ref, bias_ref, out_ref, f_ref, xs_ref, wz_ref, g_ref
):
    build_windows(x_ref, f_ref, xs_ref)
    wz_ref[...] = jnp.zeros_like(wz_ref)
    combine_weights(w_ref, wz_ref)
    total_b = products(count_ref[0], xs_ref, cot_ref, bias_ref, wz_ref, g_ref)
    for k in range(27):
        out_ref[:, k] = tap_gradient(g_ref, k).reshape(8, 16, 128)
    out_ref[:, 27] = jnp.broadcast_to(total_b.reshape(1, 1, 128), (8, 16, 128))


def terms(count, w, x, cot, bias):
    return pl.pallas_call(
        terms_kernel,
        out_shape=jax.ShapeDtypeStruct((8, 28, 16, 128), jnp.float32),
        in_specs=[pl.BlockSpec(memory_space=pltpu.SMEM)]
        + [pl.BlockSpec(memory_space=pltpu.VMEM)] * 4,
        out_specs=pl.BlockSpec(memory_space=pltpu.VMEM),
        scratch_shapes=WORK,
        compiler_params=pltpu.CompilerParams(vmem_limit_bytes=48 * 2**20),
    )(count, w, x, cot, bias)


def xor(value, mask):
    if mask == 1:
        return value + 1 - 2 * (value % 2)
    if mask == 2:
        return (value + 2) % 4
    return 3 - value


def lay_out_tiles(x_raw, f_ref, xs_ref, xt_ref):
    pad = 8
    rows = 576
    full = x_raw[...].astype(jnp.float32)
    for tf in range(36):
        for h in range(4):
            at = pad + h * 144 + tf * 4
            f_ref[2, at : at + 4] = full[tf * 16 + h * 4 : tf * 16 + h * 4 + 4]
    row = lax.broadcasted_iota(jnp.int32, (144, 128), 0)
    w = row % 4
    frame = (row // 4) % 9
    for h in range(4):
        at = pad + h * 144
        now = f_ref[2, at : at + 144]
        back1 = jnp.where(frame < 1, now, f_ref[2, at - 4 : at + 140])
        back2 = jnp.where(frame < 2, back1, f_ref[2, at - 8 : at + 136])
        f_ref[1, at : at + 144] = back1
        f_ref[0, at : at + 144] = back2
    for kd in range(3):
        for h in range(4):
            at = pad + h * 144
            lines = slice(h * 144, h * 144 + 144)
            left = jnp.where(w == 0, 0.0, f_ref[kd, at - 1 : at + 143])
            here = f_ref[kd, at : at + 144]
            right = jnp.where(w == 3, 0.0, f_ref[kd, at + 1 : at + 145])
            left, here, right = (
                piece.astype(jnp.bfloat16) for piece in (left, here, right)
            )
            col = kd * 256
            xs_ref[0, lines, col : col + 128] = left
            xs_ref[0, lines, col + 128 : col + 256] = here
            xs_ref[1, lines, col : col + 128] = here
            xs_ref[1, lines, col + 128 : col + 256] = right
    for kd in range(3):
        for pw in range(2):
            for b in range(2):
                col = kd * 256 + b * 128
                if (pw, b) == (1, 0):
                    continue
                block = xs_ref[pw, :, col : col + 128].astype(jnp.float32).T
                block = block.astype(jnp.bfloat16)
                xt_ref[pw, col : col + 128, :] = block
                if (pw, b) == (0, 1):
                    xt_ref[1, kd * 256 : kd * 256 + 128, :] = block


def lay_out_cotangent(cot_raw, cf_ref, cp_ref):
    for tf in range(36):
        full = cot_raw[tf * 64 : tf * 64 + 64].astype(jnp.float32)
        for line in range(8):
            cf_ref[line, tf * 8 : tf * 8 + 8] = full[line * 8 : line * 8 + 8]
    for h in range(4):
        for ph in range(2):
            for pw in range(2):
                cp_ref[2 * ph + pw, h * 144 : h * 144 + 144] = cf_ref[
                    2 * h + ph, pl.ds(pw, 144, 2), :
                ]


def combine_shard(w_ref, d, wz_ref):
    for kd in range(3):
        tap = {}
        for kh in range(3):
            for kw in range(3):
                tap[kh, kw] = w_ref[d, 9 * kd + 3 * kh + kw].astype(jnp.float32)
        for ph in range(2):
            for a in range(2):
                line = [sum(tap[kh, kw] for kh in TAPS[ph, a]) for kw in range(3)]
                for pw in range(2):
                    for b in range(2):
                        both = sum(line[kw] for kw in TAPS[pw, b])
                        row = pl.multiple_of(kd * 256 + b * 128 + d * 16, 16)
                        col = (2 * ph + a) * 128
                        wz_ref[pw, pl.ds(row, 16), col : col + 128] = both.astype(
                            jnp.bfloat16
                        )


def forward(count, xs_ref, wz_ref, y_ref, cp_ref, bias_ref, dz_ref):
    f32 = jnp.float32
    place = lax.broadcasted_iota(jnp.int32, (144, 128), 0)
    live = place < 36 * count
    total_b = jnp.zeros((1, 128), f32)
    for pw in range(2):
        y_ref[pw] = jnp.dot(xs_ref[pw], wz_ref[pw], preferred_element_type=f32)
    for pw in range(2):
        for ph in range(2):
            for h in range(4):
                lines = slice(h * 144, h * 144 + 144)
                col = ph * 256
                z = bias_ref[...]
                for a in range(2):
                    s = h + a + ph - 1
                    if 0 <= s < 4:
                        z = z + y_ref[
                            pw,
                            s * 144 : s * 144 + 144,
                            col + a * 128 : col + a * 128 + 128,
                        ]
                sig = 0.5 + 0.5 * jnp.tanh(0.5 * z)
                dz = cp_ref[2 * ph + pw, lines] * sig * (1.0 + z * (1.0 - sig))
                dz = jnp.where(live, dz, 0.0).astype(jnp.bfloat16)
                total_b += jnp.sum(dz.astype(f32), axis=0, keepdims=True)
                for a in range(2):
                    s = h + a + ph - 1
                    if 0 <= s < 4:
                        dz_ref[
                            pw,
                            s * 144 : s * 144 + 144,
                            col + a * 128 : col + a * 128 + 128,
                        ] = dz
    return total_b


def clear_edges(dz_ref):
    zero = jnp.zeros((144, 128), jnp.bfloat16)
    for pw in range(2):
        dz_ref[pw, 432:576, 0:128] = zero
        dz_ref[pw, 0:144, 384:512] = zero


def backward(xt_ref, dz_ref, g_ref):
    for pw in range(2):
        g_ref[pw] = jnp.dot(
            xt_ref[pw], dz_ref[pw], preferred_element_type=jnp.float32
        )


def tap_sums(g_ref, base, store):
    for kd in range(3):
        line = {}
        for pw in range(2):
            for b in range(2):
                row = pl.multiple_of(kd * 256 + b * 128 + base, 16)
                part = [
                    g_ref[pw, pl.ds(row, 16), c * 128 : c * 128 + 128]
                    for c in range(4)
                ]
                for kh in range(3):
                    line[pw, b, kh] = part[OFFSET[0][kh]] + part[2 + OFFSET[1][kh]]
        for kh in range(3):
            for kw in range(3):
                store(
                    9 * kd + 3 * kh + kw,
                    line[0, OFFSET[0][kw], kh] + line[1, OFFSET[1][kw], kh],
                )


def whole_kernel(
    scale, counts_any, w_any, x_any, cot_any, bias_any, o_ref, b_ref,
    counts_ref, w_raw, x_raw, cot_raw, bias_ref,
    wf_ref, f_ref, cf_ref, cp_ref, xs_ref, xt_ref, wz_ref, y_ref, dz_ref, g_ref,
    w_all, parts, s1, r1, s2, r2, keep, s3, r3, last, sb, rb,
    fetch, sw3, rw3, sw1, rw1, sw2, rw2, ss1, rs1, ss2, rs2, ss3, rs3, ss4, rs4, ssb, rsb,
):
    grp = lax.axis_index("grp")
    dev = lax.axis_index("dev")
    depth = dev // 2
    core = dev % 2
    f32, bf16 = jnp.float32, jnp.bfloat16
    masks = (3, 2, 1)
    pair = {"dev": depth * 2 + (1 - core)}
    across = [{"grp": xor(grp, m)} for m in masks]
    along = [{"dev": xor(depth, m) * 2 + core} for m in masks]

    fetches = []
    for i, (src, dst) in enumerate(
        (
            (w_any, w_raw),
            (cot_any, cot_raw),
            (x_any, x_raw),
            (bias_any, bias_ref),
            (counts_any, counts_ref),
        )
    ):
        fetches.append(pltpu.make_async_copy(src, dst, fetch.at[i]))
        fetches[i].start()

    barrier = pltpu.get_barrier_semaphore()
    for peer in [pair] + across + along:
        pl.semaphore_signal(barrier, inc=1, device_id=peer, device_id_type=MESH)

    def send(src, dst, ssem, rsem, peer):
        copy = pltpu.make_async_remote_copy(
            src_ref=src, dst_ref=dst, send_sem=ssem, recv_sem=rsem,
            device_id=peer, device_id_type=MESH,
        )
        copy.start()
        return copy

    fetches[0].wait()
    wf_ref[...] = w_raw[...].astype(f32)
    for k in range(27):
        w_all[dev, k] = wf_ref[pl.ds(k, 16, 27), :].astype(bf16)
    w_all[dev, 27] = jnp.zeros((16, 128), bf16)
    pl.semaphore_wait(barrier, 7)

    quarter = pl.ds(grp * 7, 7)
    out = [
        send(w_all.at[dev, quarter], w_all.at[dev, quarter], sw1.at[k], rw1.at[k], along[k])
        for k in range(3)
    ]
    swap = [send(w_all.at[dev], w_all.at[dev], sw2.at[3], rw2.at[3], pair)]
    clear_edges(dz_ref)
    zero = jnp.zeros((16, 128), bf16)
    for k in range(4):
        s1[k, 27] = zero
        parts[k, 27] = jnp.zeros((16, 128), f32)
    combine_shard(w_all, dev, wz_ref)
    fetches[1].wait()
    lay_out_cotangent(cot_raw, cf_ref, cp_ref)
    spread = {}
    for k in (2, 1, 0):
        out[k].wait_recv()
        block = w_all.at[xor(depth, masks[k]) * 2 + core, quarter]
        for j in range(3):
            spread[k, j] = send(block, block, sw3.at[k, j], rw3.at[k, j], across[j])
    fetches[2].wait()
    lay_out_tiles(x_raw, f_ref, xs_ref, xt_ref)
    swap[0].wait_recv()
    combine_shard(w_all, depth * 2 + 1 - core, wz_ref)
    for k in (2, 1, 0):
        for j in range(3):
            spread[k, j].wait_recv()
        block = w_all.at[xor(depth, masks[k]) * 2 + core]
        swap.append(send(block, block, sw2.at[k], rw2.at[k], pair))
        combine_shard(w_all, xor(depth, masks[k]) * 2 + core, wz_ref)
    for i, k in enumerate((2, 1, 0)):
        swap[1 + i].wait_recv()
        combine_shard(w_all, xor(depth, masks[k]) * 2 + 1 - core, wz_ref)
    fetches[3].wait()
    fetches[4].wait()
    total_b = forward(
        counts_ref[grp * 8 + dev], xs_ref, wz_ref, y_ref, cp_ref, bias_ref, dz_ref
    )

    sb[0] = jnp.broadcast_to(total_b, (8, 128))
    bias_copies = [send(sb.at[0], rb.at[0], ssb.at[0], rsb.at[0], pair)]
    backward(xt_ref, dz_ref, g_ref)
    first, second, third = [], [], []
    ahead = (3, 2, 1, 0)

    def start_first(k):
        base = (xor(depth, ahead[k]) if ahead[k] else depth) * 32

        def to_pair(tap, value):
            s1[k, tap] = value.astype(bf16)

        def to_self(tap, value):
            parts[k, tap] = value

        tap_sums(g_ref, base + (1 - core) * 16, to_pair)
        first.append(send(s1.at[k], r1.at[k], ss1.at[k], rs1.at[k], pair))
        tap_sums(g_ref, base + core * 16, to_self)

    def start_second(k):
        first[k].wait_recv()
        for j in range(4):
            owner = xor(grp, masks[j]) if j < 3 else grp
            taps = pl.ds(owner * 7, 7)
            total = parts[k, taps] + r1[k, taps].astype(f32)
            if j < 3:
                s2[k, j] = total.astype(bf16)
                second.append(
                    send(s2.at[k, j], r2.at[k, j], ss2.at[k, j], rs2.at[k, j], across[j])
                )
            else:
                keep[k] = total

    def start_third(k):
        total = keep[k]
        for j in range(3):
            second[3 * k + j].wait_recv()
            total += r2[k, j].astype(f32)
        if k < 3:
            s3[k] = total.astype(bf16)
            third.append(send(s3.at[k], r3.at[k], ss3.at[k], rs3.at[k], along[k]))
        else:
            keep[k] = total

    start_first(0)
    start_first(1)
    start_second(0)
    start_first(2)
    start_second(1)
    start_first(3)
    start_second(2)
    start_second(3)
    bias_copies[0].wait_recv()
    sb[1] = sb[0] + rb[0]
    for k in range(3):
        bias_copies.append(
            send(sb.at[1], rb.at[1 + k], ssb.at[1 + k], rsb.at[1 + k], across[k])
        )
    start_third(0)
    start_third(1)
    start_third(2)
    for k in range(3):
        bias_copies[1 + k].wait_recv()
    sb[2] = (sb[1] + rb[3]) + (rb[2] + rb[1])
    for k in range(3):
        bias_copies.append(
            send(sb.at[2], rb.at[4 + k], ssb.at[4 + k], rsb.at[4 + k], along[k])
        )
    start_third(3)
    total = keep[3]
    for k in (2, 1, 0):
        third[k].wait_recv()
        total += r3[k].astype(f32)
    last[grp] = (total * scale).astype(bf16)
    fourth = [
        send(last.at[grp], last.at[grp], ss4.at[k], rs4.at[k], across[k])
        for k in range(3)
    ]
    for k in range(3):
        bias_copies[4 + k].wait_recv()
    total_b = (((sb[2] + rb[6]) + (rb[5] + rb[4])) * scale)[0:1]
    mine = jnp.zeros((1, 16), f32)
    for d in range(8):
        mine = jnp.where(dev == d, total_b[:, d * 16 : d * 16 + 16], mine)
    b_ref[...] = mine
    for k in (2, 1, 0):
        fourth[k].wait_recv()
    for k in range(27):
        o_ref[pl.ds(k, 16, 27), :] = last[k // 7, k % 7].astype(f32)
    for copy in out + list(spread.values()) + swap + bias_copies + first + second + third + fourth:
        copy.wait_send()


def whole(counts, w, x, cot, bias, scale):
    bf16, f32 = jnp.bfloat16, jnp.float32
    sem = pltpu.SemaphoreType.DMA
    vmem = pltpu.VMEM
    return pl.pallas_call(
        functools.partial(whole_kernel, scale),
        out_shape=(
            jax.ShapeDtypeStruct((432, 128), f32),
            jax.ShapeDtypeStruct((1, 16), f32),
        ),
        in_specs=[pl.BlockSpec(memory_space=pltpu.HBM)] * 5,
        out_specs=[pl.BlockSpec(memory_space=pltpu.VMEM)] * 2,
        scratch_shapes=[
            pltpu.SMEM((32,), jnp.int32),
            vmem((432, 128), bf16),
            vmem((576, 128), bf16),
            vmem((2304, 128), bf16),
            vmem((1, 128), f32),
            vmem((432, 128), f32),
            vmem((3, 592, 128), f32),
            vmem((8, 288, 128), f32),
            vmem((4, 576, 128), f32),
            vmem((2, 576, 768), bf16),
            vmem((2, 768, 576), bf16),
            vmem((2, 768, 512), bf16),
            vmem((2, 576, 512), f32),
            vmem((2, 576, 512), bf16),
            vmem((2, 768, 512), f32),
            vmem((8, 28, 16, 128), bf16),
            vmem((4, 28, 16, 128), f32),
            vmem((4, 28, 16, 128), bf16),
            vmem((4, 28, 16, 128), bf16),
            vmem((4, 3, 7, 16, 128), bf16),
            vmem((4, 3, 7, 16, 128), bf16),
            vmem((4, 7, 16, 128), f32),
            vmem((3, 7, 16, 128), bf16),
            vmem((3, 7, 16, 128), bf16),
            vmem((4, 7, 16, 128), bf16),
            vmem((3, 8, 128), f32),
            vmem((7, 8, 128), f32),
            sem((5,)), sem((3, 3)), sem((3, 3)),
            sem((3,)), sem((3,)), sem((4,)), sem((4,)),
            sem((4,)), sem((4,)), sem((4, 3)), sem((4, 3)),
            sem((3,)), sem((3,)), sem((3,)), sem((3,)),
            sem((7,)), sem((7,)),
        ],
        compiler_params=pltpu.CompilerParams(
            collective_id=1, has_side_effects=True, vmem_limit_bytes=48 * 2**20
        ),
    )(counts, w, x, cot, bias)


def body(tiles, cotangent, weight, bias, counts):
    num_dev = lax.axis_size("dev")
    num_grp = lax.axis_size("grp")
    cap, frames, hl, wl, cin = tiles.shape
    cout = weight.shape[1]
    my_dev = lax.axis_index("dev")
    my_grp = lax.axis_index("grp")
    scale = 1.0 / math.sqrt(cap * num_dev * num_grp * frames * 4 * hl * wl)
    bias = bias.reshape(1, cout)
    if (num_grp, num_dev) == (4, 8):
        x = tiles.reshape(cap * frames * hl * wl, cin)
        cot = cotangent.reshape(cap * frames * 4 * hl * wl, cout)
        part_w, part_b = whole(counts, weight, x, cot, bias, scale)
        return part_w, part_b.reshape(cout // num_dev)

    mine = weight.reshape(cin // num_dev, 27, cout).transpose(1, 0, 2)
    x = tiles.transpose(2, 3, 0, 1, 4).reshape(hl * wl * cap * frames, cin)
    cot = cotangent.reshape(cap, frames, hl, 2, wl, 2, cout).transpose(3, 5, 2, 4, 0, 1, 6)
    cot = cot.reshape(4, hl * wl * cap * frames, cout)
    share = cout // num_dev
    gathered = lax.all_gather(mine, "dev", axis=0, tiled=False)
    if num_dev != 8:
        gathered = gathered.transpose(1, 0, 2, 3).reshape(27, 8, 16, cout)
        gathered = gathered.transpose(1, 0, 2, 3)
    count = lax.dynamic_slice_in_dim(counts, my_grp * num_dev + my_dev, 1)
    parts = terms(count, gathered, x, cot, bias)
    flat = parts[:, :27].transpose(0, 2, 1, 3).reshape(cin * 27, cout)
    part_w = lax.psum_scatter(flat, "dev", scatter_dimension=0, tiled=True)
    part_w = lax.psum(part_w, "grp")
    total_b = lax.psum(parts[0, 27, 0], ("grp", "dev"))
    part_b = lax.dynamic_slice_in_dim(total_b, my_dev * share, share, 0)
    return part_w * scale, part_b * scale


def solution(mesh):
    return jax.shard_map(
        body,
        mesh=mesh,
        in_specs=(
            P(("grp", "dev"), None, None, None, None),
            P(("grp", "dev"), None, None, None, None),
            P("dev", None),
            P(),
            P(),
        ),
        out_specs=(P("dev", None), P("dev")),
        check_vma=False,
    )
```

```python
import functools
import math

import jax
import jax.numpy as jnp
from jax import lax
from jax.experimental import pallas as pl
from jax.experimental.pallas import tpu as pltpu
from jax.sharding import PartitionSpec as P

MESH = pl.DeviceIdType.MESH
TAPS = {(0, 0): (0,), (0, 1): (1, 2), (1, 0): (0, 1), (1, 1): (2,)}
OFFSET = ((0, 1, 1), (0, 0, 1))


def build_windows(x_ref, f_ref, xs_ref):
    rows = x_ref.shape[0]
    slab = rows // 4
    pad = 40
    row = lax.broadcasted_iota(jnp.int32, (rows, 128), 0).astype(jnp.float32)
    frame = row - 9.0 * jnp.floor((row + 0.5) * (1.0 / 9.0))
    place = lax.broadcasted_iota(jnp.int32, (slab, 128), 0)
    xs_ref[0:slab] = jnp.zeros((slab, 1152), jnp.bfloat16)
    xs_ref[5 * slab : 6 * slab] = jnp.zeros((slab, 1152), jnp.bfloat16)
    f_ref[...] = jnp.zeros_like(f_ref)
    now = x_ref[...].astype(jnp.float32)
    f_ref[2, pad : pad + rows] = now
    back1 = jnp.where(frame < 0.5, now, f_ref[2, pad - 1 : pad - 1 + rows])
    f_ref[1, pad : pad + rows] = back1
    f_ref[0, pad : pad + rows] = jnp.where(
        frame < 1.5, back1, f_ref[2, pad - 2 : pad - 2 + rows]
    )
    for h in range(4):
        for dw in range(3):
            for kd in range(3):
                start = pad + h * slab + (dw - 1) * 36
                piece = f_ref[kd, start : start + slab]
                if dw == 0:
                    piece = jnp.where(place < 36, 0.0, piece)
                if dw == 2:
                    piece = jnp.where(place >= slab - 36, 0.0, piece)
                col = dw * 384 + kd * 128
                xs_ref[(h + 1) * slab : (h + 2) * slab, col : col + 128] = piece.astype(
                    jnp.bfloat16
                )


def combine_weights(w_ref, wz_ref):
    chans = 128
    for kd in range(3):
        tap = {}
        for kh in range(3):
            for kw in range(3):
                piece = w_ref[:, 9 * kd + 3 * kh + kw]
                tap[kh, kw] = piece.reshape(chans, chans).astype(jnp.float32)
        for ph in range(2):
            for a in range(2):
                line = [sum(tap[kh, kw] for kh in TAPS[ph, a]) for kw in range(3)]
                for pw in range(2):
                    for b in range(2):
                        both = sum(line[kw] for kw in TAPS[pw, b])
                        row = (b + pw) * 384 + kd * 128
                        col = (2 * ph + pw) * 128
                        wz_ref[a + ph, row : row + 128, col : col + 128] = both.astype(
                            jnp.bfloat16
                        )


def products(count, xs_ref, cot_ref, bias_ref, wz_ref, g_ref):
    slab = xs_ref.shape[0] // 6
    rows = 4 * slab
    row = lax.broadcasted_iota(jnp.int32, (rows, 128), 0).astype(jnp.float32)
    place = row - 36.0 * jnp.floor((row + 0.5) * (1.0 / 36.0))
    live = place < 9.0 * count.astype(jnp.float32)
    cols = ((0, 256), (0, 512), (256, 256))

    def window(dh):
        return xs_ref[dh * slab : dh * slab + rows, :]

    mid = jnp.dot(window(1), wz_ref[1], preferred_element_type=jnp.float32)
    top = jnp.dot(window(0), wz_ref[0, :, 0:256], preferred_element_type=jnp.float32)
    low = jnp.dot(window(2), wz_ref[2, :, 256:512], preferred_element_type=jnp.float32)
    parts = []
    total_b = jnp.zeros((1, 128), jnp.float32)
    for p in range(4):
        side = (top if p < 2 else low)[:, (p % 2) * 128 : (p % 2) * 128 + 128]
        z = mid[:, p * 128 : p * 128 + 128] + side + bias_ref[...]
        sig = jax.nn.sigmoid(z)
        dz = cot_ref[p].astype(jnp.float32) * sig * (1.0 + z * (1.0 - sig))
        dz = jnp.where(live, dz, 0.0).astype(jnp.bfloat16)
        total_b += jnp.sum(dz.astype(jnp.float32), axis=0, keepdims=True)
        parts.append(dz)
    dz = jnp.concatenate(parts, axis=1)
    for dh in range(3):
        start, width = cols[dh]
        g_ref[dh, :, start : start + width] = lax.dot_general(
            window(dh),
            dz[:, start : start + width],
            (((0,), (0,)), ((), ())),
            preferred_element_type=jnp.float32,
        )
    return total_b


def tap_gradient(g_ref, k, base=0, size=128):
    kd, kh, kw = k // 9, k // 3 % 3, k % 3
    total = None
    for ph in range(2):
        for pw in range(2):
            row = (OFFSET[pw][kw] + pw) * 384 + kd * 128
            col = (2 * ph + pw) * 128
            term = g_ref[
                OFFSET[ph][kh] + ph, pl.ds(base + row, size), col : col + 128
            ]
            total = term if total is None else total + term
    return total


WORK = [
    pltpu.VMEM((3, 656, 128), jnp.float32),
    pltpu.VMEM((864, 1152), jnp.bfloat16),
    pltpu.VMEM((3, 1152, 512), jnp.bfloat16),
    pltpu.VMEM((3, 1152, 512), jnp.float32),
]


def terms_kernel(
    count_ref, w_ref, x_ref, cot_ref, bias_ref, out_ref, f_ref, xs_ref, wz_ref, g_ref
):
    build_windows(x_ref, f_ref, xs_ref)
    wz_ref[...] = jnp.zeros_like(wz_ref)
    combine_weights(w_ref, wz_ref)
    total_b = products(count_ref[0], xs_ref, cot_ref, bias_ref, wz_ref, g_ref)
    for k in range(27):
        out_ref[:, k] = tap_gradient(g_ref, k).reshape(8, 16, 128)
    out_ref[:, 27] = jnp.broadcast_to(total_b.reshape(1, 1, 128), (8, 16, 128))


def terms(count, w, x, cot, bias):
    return pl.pallas_call(
        terms_kernel,
        out_shape=jax.ShapeDtypeStruct((8, 28, 16, 128), jnp.float32),
        in_specs=[pl.BlockSpec(memory_space=pltpu.SMEM)]
        + [pl.BlockSpec(memory_space=pltpu.VMEM)] * 4,
        out_specs=pl.BlockSpec(memory_space=pltpu.VMEM),
        scratch_shapes=WORK,
        compiler_params=pltpu.CompilerParams(vmem_limit_bytes=48 * 2**20),
    )(count, w, x, cot, bias)


def xor(value, mask):
    if mask == 1:
        return value + 1 - 2 * (value % 2)
    if mask == 2:
        return (value + 2) % 4
    return 3 - value


def lay_out_tiles(x_raw, f_ref, xs_ref, xt_ref):
    pad = 8
    rows = 576
    full = x_raw[...].astype(jnp.float32)
    for tf in range(36):
        for h in range(4):
            at = pad + h * 144 + tf * 4
            f_ref[2, at : at + 4] = full[tf * 16 + h * 4 : tf * 16 + h * 4 + 4]
    row = lax.broadcasted_iota(jnp.int32, (144, 128), 0)
    w = row % 4
    frame = (row // 4) % 9
    for h in range(4):
        at = pad + h * 144
        now = f_ref[2, at : at + 144]
        back1 = jnp.where(frame < 1, now, f_ref[2, at - 4 : at + 140])
        back2 = jnp.where(frame < 2, back1, f_ref[2, at - 8 : at + 136])
        f_ref[1, at : at + 144] = back1
        f_ref[0, at : at + 144] = back2
    for kd in range(3):
        for h in range(4):
            at = pad + h * 144
            lines = slice(h * 144, h * 144 + 144)
            left = jnp.where(w == 0, 0.0, f_ref[kd, at - 1 : at + 143])
            here = f_ref[kd, at : at + 144]
            right = jnp.where(w == 3, 0.0, f_ref[kd, at + 1 : at + 145])
            left, here, right = (
                piece.astype(jnp.bfloat16) for piece in (left, here, right)
            )
            col = kd * 256
            xs_ref[0, lines, col : col + 128] = left
            xs_ref[0, lines, col + 128 : col + 256] = here
            xs_ref[1, lines, col : col + 128] = here
            xs_ref[1, lines, col + 128 : col + 256] = right
    for kd in range(3):
        for pw in range(2):
            for b in range(2):
                col = kd * 256 + b * 128
                if (pw, b) == (1, 0):
                    continue
                block = xs_ref[pw, :, col : col + 128].astype(jnp.float32).T
                block = block.astype(jnp.bfloat16)
                xt_ref[pw, col : col + 128, :] = block
                if (pw, b) == (0, 1):
                    xt_ref[1, kd * 256 : kd * 256 + 128, :] = block


def lay_out_cotangent(cot_raw, cf_ref, cp_ref):
    for tf in range(36):
        full = cot_raw[tf * 64 : tf * 64 + 64].astype(jnp.float32)
        for line in range(8):
            cf_ref[line, tf * 8 : tf * 8 + 8] = full[line * 8 : line * 8 + 8]
    for h in range(4):
        for ph in range(2):
            for pw in range(2):
                cp_ref[2 * ph + pw, h * 144 : h * 144 + 144] = cf_ref[
                    2 * h + ph, pl.ds(pw, 144, 2), :
                ]


def combine_shard(w_ref, d, wz_ref):
    for kd in range(3):
        tap = {}
        for kh in range(3):
            for kw in range(3):
                tap[kh, kw] = w_ref[d, 9 * kd + 3 * kh + kw].astype(jnp.float32)
        for ph in range(2):
            for a in range(2):
                line = [sum(tap[kh, kw] for kh in TAPS[ph, a]) for kw in range(3)]
                for pw in range(2):
                    for b in range(2):
                        both = sum(line[kw] for kw in TAPS[pw, b])
                        row = pl.multiple_of(kd * 256 + b * 128 + d * 16, 16)
                        col = (2 * ph + a) * 128
                        wz_ref[pw, pl.ds(row, 16), col : col + 128] = both.astype(
                            jnp.bfloat16
                        )


def forward(count, xs_ref, wz_ref, y_ref, cp_ref, bias_ref, dz_ref):
    f32 = jnp.float32
    place = lax.broadcasted_iota(jnp.int32, (144, 128), 0)
    live = place < 36 * count
    total_b = jnp.zeros((1, 128), f32)
    for pw in range(2):
        y_ref[pw] = jnp.dot(xs_ref[pw], wz_ref[pw], preferred_element_type=f32)
    for pw in range(2):
        for ph in range(2):
            for h in range(4):
                lines = slice(h * 144, h * 144 + 144)
                col = ph * 256
                z = bias_ref[...]
                for a in range(2):
                    s = h + a + ph - 1
                    if 0 <= s < 4:
                        z = z + y_ref[
                            pw,
                            s * 144 : s * 144 + 144,
                            col + a * 128 : col + a * 128 + 128,
                        ]
                sig = 0.5 + 0.5 * jnp.tanh(0.5 * z)
                dz = cp_ref[2 * ph + pw, lines] * sig * (1.0 + z * (1.0 - sig))
                dz = jnp.where(live, dz, 0.0).astype(jnp.bfloat16)
                total_b += jnp.sum(dz.astype(f32), axis=0, keepdims=True)
                for a in range(2):
                    s = h + a + ph - 1
                    if 0 <= s < 4:
                        dz_ref[
                            pw,
                            s * 144 : s * 144 + 144,
                            col + a * 128 : col + a * 128 + 128,
                        ] = dz
    return total_b


def clear_edges(dz_ref):
    zero = jnp.zeros((144, 128), jnp.bfloat16)
    for pw in range(2):
        dz_ref[pw, 432:576, 0:128] = zero
        dz_ref[pw, 0:144, 384:512] = zero


def backward(xt_ref, dz_ref, g_ref):
    for pw in range(2):
        g_ref[pw] = jnp.dot(
            xt_ref[pw], dz_ref[pw], preferred_element_type=jnp.float32
        )


def tap_sums(g_ref, base, store):
    for kd in range(3):
        line = {}
        for pw in range(2):
            for b in range(2):
                row = pl.multiple_of(kd * 256 + b * 128 + base, 16)
                part = [
                    g_ref[pw, pl.ds(row, 16), c * 128 : c * 128 + 128]
                    for c in range(4)
                ]
                for kh in range(3):
                    line[pw, b, kh] = part[OFFSET[0][kh]] + part[2 + OFFSET[1][kh]]
        for kh in range(3):
            for kw in range(3):
                store(
                    9 * kd + 3 * kh + kw,
                    line[0, OFFSET[0][kw], kh] + line[1, OFFSET[1][kw], kh],
                )


def whole_kernel(
    scale, counts_any, w_any, x_any, cot_any, bias_any, o_ref, b_ref,
    counts_ref, w_raw, x_raw, cot_raw, bias_ref,
    wf_ref, f_ref, cf_ref, cp_ref, xs_ref, xt_ref, wz_ref, y_ref, dz_ref, g_ref,
    w_all, parts, s1, r1, s2, r2, keep, s3, r3, last, sb, rb,
    fetch, sw3, rw3, sw1, rw1, sw2, rw2, ss1, rs1, ss2, rs2, ss3, rs3, ss4, rs4, ssb, rsb,
):
    grp = lax.axis_index("grp")
    dev = lax.axis_index("dev")
    depth = dev // 2
    core = dev % 2
    f32, bf16 = jnp.float32, jnp.bfloat16
    masks = (3, 2, 1)
    pair = {"dev": depth * 2 + (1 - core)}
    across = [{"grp": xor(grp, m)} for m in masks]
    along = [{"dev": xor(depth, m) * 2 + core} for m in masks]

    fetches = []
    for i, (src, dst) in enumerate(
        (
            (w_any, w_raw),
            (cot_any, cot_raw),
            (x_any, x_raw),
            (bias_any, bias_ref),
            (counts_any, counts_ref),
        )
    ):
        fetches.append(pltpu.make_async_copy(src, dst, fetch.at[i]))
        fetches[i].start()

    barrier = pltpu.get_barrier_semaphore()
    for peer in [pair] + across + along:
        pl.semaphore_signal(barrier, inc=1, device_id=peer, device_id_type=MESH)

    def send(src, dst, ssem, rsem, peer):
        copy = pltpu.make_async_remote_copy(
            src_ref=src, dst_ref=dst, send_sem=ssem, recv_sem=rsem,
            device_id=peer, device_id_type=MESH,
        )
        copy.start()
        return copy

    fetches[0].wait()
    wf_ref[...] = w_raw[...].astype(f32)
    for k in range(27):
        w_all[dev, k] = wf_ref[pl.ds(k, 16, 27), :].astype(bf16)
    w_all[dev, 27] = jnp.zeros((16, 128), bf16)
    pl.semaphore_wait(barrier, 7)

    quarter = pl.ds(grp * 7, 7)
    out = [
        send(w_all.at[dev, quarter], w_all.at[dev, quarter], sw1.at[k], rw1.at[k], along[k])
        for k in range(3)
    ]
    swap = [send(w_all.at[dev], w_all.at[dev], sw2.at[3], rw2.at[3], pair)]
    clear_edges(dz_ref)
    zero = jnp.zeros((16, 128), bf16)
    for k in range(4):
        s1[k, 27] = zero
        parts[k, 27] = jnp.zeros((16, 128), f32)
    combine_shard(w_all, dev, wz_ref)
    fetches[1].wait()
    lay_out_cotangent(cot_raw, cf_ref, cp_ref)
    spread = {}
    for k in (2, 1, 0):
        out[k].wait_recv()
        block = w_all.at[xor(depth, masks[k]) * 2 + core, quarter]
        for j in range(3):
            spread[k, j] = send(block, block, sw3.at[k, j], rw3.at[k, j], across[j])
    fetches[2].wait()
    lay_out_tiles(x_raw, f_ref, xs_ref, xt_ref)
    swap[0].wait_recv()
    combine_shard(w_all, depth * 2 + 1 - core, wz_ref)
    for k in (2, 1, 0):
        for j in range(3):
            spread[k, j].wait_recv()
        block = w_all.at[xor(depth, masks[k]) * 2 + core]
        swap.append(send(block, block, sw2.at[k], rw2.at[k], pair))
        combine_shard(w_all, xor(depth, masks[k]) * 2 + core, wz_ref)
    for i, k in enumerate((2, 1, 0)):
        swap[1 + i].wait_recv()
        combine_shard(w_all, xor(depth, masks[k]) * 2 + 1 - core, wz_ref)
    fetches[3].wait()
    fetches[4].wait()
    total_b = forward(
        counts_ref[grp * 8 + dev], xs_ref, wz_ref, y_ref, cp_ref, bias_ref, dz_ref
    )

    sb[0] = jnp.broadcast_to(total_b, (8, 128))
    bias_copies = [send(sb.at[0], rb.at[0], ssb.at[0], rsb.at[0], pair)]
    backward(xt_ref, dz_ref, g_ref)
    first, second, third = [], [], []
    ahead = (3, 2, 1, 0)

    def start_first(k):
        base = (xor(depth, ahead[k]) if ahead[k] else depth) * 32

        def to_pair(tap, value):
            s1[k, tap] = value.astype(bf16)

        def to_self(tap, value):
            parts[k, tap] = value

        tap_sums(g_ref, base + (1 - core) * 16, to_pair)
        first.append(send(s1.at[k], r1.at[k], ss1.at[k], rs1.at[k], pair))
        tap_sums(g_ref, base + core * 16, to_self)

    def start_second(k):
        first[k].wait_recv()
        for j in range(4):
            owner = xor(grp, masks[j]) if j < 3 else grp
            taps = pl.ds(owner * 7, 7)
            total = parts[k, taps] + r1[k, taps].astype(f32)
            if j < 3:
                s2[k, j] = total.astype(bf16)
                second.append(
                    send(s2.at[k, j], r2.at[k, j], ss2.at[k, j], rs2.at[k, j], across[j])
                )
            else:
                keep[k] = total

    def start_third(k):
        total = keep[k]
        for j in range(3):
            second[3 * k + j].wait_recv()
            total += r2[k, j].astype(f32)
        if k < 3:
            s3[k] = total.astype(bf16)
            third.append(send(s3.at[k], r3.at[k], ss3.at[k], rs3.at[k], along[k]))
        else:
            keep[k] = total

    start_first(0)
    start_first(1)
    start_second(0)
    start_first(2)
    start_second(1)
    start_first(3)
    start_second(2)
    start_second(3)
    bias_copies[0].wait_recv()
    sb[1] = sb[0] + rb[0]
    for k in range(3):
        bias_copies.append(
            send(sb.at[1], rb.at[1 + k], ssb.at[1 + k], rsb.at[1 + k], across[k])
        )
    start_third(0)
    start_third(1)
    start_third(2)
    for k in range(3):
        bias_copies[1 + k].wait_recv()
    sb[2] = (sb[1] + rb[3]) + (rb[2] + rb[1])
    for k in range(3):
        bias_copies.append(
            send(sb.at[2], rb.at[4 + k], ssb.at[4 + k], rsb.at[4 + k], along[k])
        )
    start_third(3)
    total = keep[3]
    for k in (2, 1, 0):
        third[k].wait_recv()
        total += r3[k].astype(f32)
    last[grp] = (total * scale).astype(bf16)
    fourth = [
        send(last.at[grp], last.at[grp], ss4.at[k], rs4.at[k], across[k])
        for k in range(3)
    ]
    for k in range(3):
        bias_copies[4 + k].wait_recv()
    total_b = (((sb[2] + rb[6]) + (rb[5] + rb[4])) * scale)[0:1]
    mine = jnp.zeros((1, 16), f32)
    for d in range(8):
        mine = jnp.where(dev == d, total_b[:, d * 16 : d * 16 + 16], mine)
    b_ref[...] = mine
    for k in (2, 1, 0):
        fourth[k].wait_recv()
    for k in range(27):
        o_ref[pl.ds(k, 16, 27), :] = last[k // 7, k % 7].astype(f32)
    for copy in out + list(spread.values()) + swap + bias_copies + first + second + third + fourth:
        copy.wait_send()


def whole(counts, w, x, cot, bias, scale):
    bf16, f32 = jnp.bfloat16, jnp.float32
    sem = pltpu.SemaphoreType.DMA
    vmem = pltpu.VMEM
    return pl.pallas_call(
        functools.partial(whole_kernel, scale),
        out_shape=(
            jax.ShapeDtypeStruct((432, 128), f32),
            jax.ShapeDtypeStruct((1, 16), f32),
        ),
        in_specs=[pl.BlockSpec(memory_space=pltpu.HBM)] * 5,
        out_specs=[pl.BlockSpec(memory_space=pltpu.VMEM)] * 2,
        scratch_shapes=[
            pltpu.SMEM((32,), jnp.int32),
            vmem((432, 128), bf16),
            vmem((576, 128), bf16),
            vmem((2304, 128), bf16),
            vmem((1, 128), f32),
            vmem((432, 128), f32),
            vmem((3, 592, 128), f32),
            vmem((8, 288, 128), f32),
            vmem((4, 576, 128), f32),
            vmem((2, 576, 768), bf16),
            vmem((2, 768, 576), bf16),
            vmem((2, 768, 512), bf16),
            vmem((2, 576, 512), f32),
            vmem((2, 576, 512), bf16),
            vmem((2, 768, 512), f32),
            vmem((8, 28, 16, 128), bf16),
            vmem((4, 28, 16, 128), f32),
            vmem((4, 28, 16, 128), bf16),
            vmem((4, 28, 16, 128), bf16),
            vmem((4, 3, 7, 16, 128), bf16),
            vmem((4, 3, 7, 16, 128), bf16),
            vmem((4, 7, 16, 128), f32),
            vmem((3, 7, 16, 128), bf16),
            vmem((3, 7, 16, 128), bf16),
            vmem((4, 7, 16, 128), bf16),
            vmem((3, 8, 128), f32),
            vmem((7, 8, 128), f32),
            sem((5,)), sem((3, 3)), sem((3, 3)),
            sem((3,)), sem((3,)), sem((4,)), sem((4,)),
            sem((4,)), sem((4,)), sem((4, 3)), sem((4, 3)),
            sem((3,)), sem((3,)), sem((3,)), sem((3,)),
            sem((7,)), sem((7,)),
        ],
        compiler_params=pltpu.CompilerParams(
            collective_id=1, has_side_effects=True, vmem_limit_bytes=60 * 2**20
        ),
    )(counts, w, x, cot, bias)


def hand_on_kernel(w_ref, b_ref, o_any, p_any, sems):
    copies = [
        pltpu.make_async_copy(w_ref, o_any, sems.at[0]),
        pltpu.make_async_copy(b_ref, p_any, sems.at[1]),
    ]
    for copy in copies:
        copy.start()
    for copy in copies:
        copy.wait()


def hand_on(part_w, part_b):
    return pl.pallas_call(
        hand_on_kernel,
        out_shape=(
            jax.ShapeDtypeStruct(part_w.shape, part_w.dtype),
            jax.ShapeDtypeStruct(part_b.shape, part_b.dtype),
        ),
        in_specs=[pl.BlockSpec(memory_space=pltpu.VMEM)] * 2,
        out_specs=[pl.BlockSpec(memory_space=pltpu.HBM)] * 2,
        scratch_shapes=[pltpu.SemaphoreType.DMA((2,))],
    )(part_w, part_b)


def body(tiles, cotangent, weight, bias, counts):
    num_dev = lax.axis_size("dev")
    num_grp = lax.axis_size("grp")
    cap, frames, hl, wl, cin = tiles.shape
    cout = weight.shape[1]
    my_dev = lax.axis_index("dev")
    my_grp = lax.axis_index("grp")
    scale = 1.0 / math.sqrt(cap * num_dev * num_grp * frames * 4 * hl * wl)
    bias = bias.reshape(1, cout)
    if (num_grp, num_dev) == (4, 8):
        x = tiles.reshape(cap * frames * hl * wl, cin)
        cot = cotangent.reshape(cap * frames * 4 * hl * wl, cout)
        part_w, part_b = hand_on(*whole(counts, weight, x, cot, bias, scale))
        return part_w, part_b.reshape(cout // num_dev)

    mine = weight.reshape(cin // num_dev, 27, cout).transpose(1, 0, 2)
    x = tiles.transpose(2, 3, 0, 1, 4).reshape(hl * wl * cap * frames, cin)
    cot = cotangent.reshape(cap, frames, hl, 2, wl, 2, cout).transpose(3, 5, 2, 4, 0, 1, 6)
    cot = cot.reshape(4, hl * wl * cap * frames, cout)
    share = cout // num_dev
    gathered = lax.all_gather(mine, "dev", axis=0, tiled=False)
    if num_dev != 8:
        gathered = gathered.transpose(1, 0, 2, 3).reshape(27, 8, 16, cout)
        gathered = gathered.transpose(1, 0, 2, 3)
    count = lax.dynamic_slice_in_dim(counts, my_grp * num_dev + my_dev, 1)
    parts = terms(count, gathered, x, cot, bias)
    flat = parts[:, :27].transpose(0, 2, 1, 3).reshape(cin * 27, cout)
    part_w = lax.psum_scatter(flat, "dev", scatter_dimension=0, tiled=True)
    part_w = lax.psum(part_w, "grp")
    total_b = lax.psum(parts[0, 27, 0], ("grp", "dev"))
    part_b = lax.dynamic_slice_in_dim(total_b, my_dev * share, share, 0)
    return part_w * scale, part_b * scale


def solution(mesh):
    return jax.shard_map(
        body,
        mesh=mesh,
        in_specs=(
            P(("grp", "dev"), None, None, None, None),
            P(("grp", "dev"), None, None, None, None),
            P("dev", None),
            P(),
            P(),
        ),
        out_specs=(P("dev", None), P("dev")),
        check_vma=False,
    )
```

```python
import functools
import math

import jax
import jax.numpy as jnp
from jax import lax
from jax.experimental import pallas as pl
from jax.experimental.pallas import tpu as pltpu
from jax.sharding import PartitionSpec as P

MESH = pl.DeviceIdType.MESH
TAPS = {(0, 0): (0,), (0, 1): (1, 2), (1, 0): (0, 1), (1, 1): (2,)}
OFFSET = ((0, 1, 1), (0, 0, 1))


def build_windows(x_ref, f_ref, xs_ref):
    rows = x_ref.shape[0]
    slab = rows // 4
    pad = 40
    row = lax.broadcasted_iota(jnp.int32, (rows, 128), 0).astype(jnp.float32)
    frame = row - 9.0 * jnp.floor((row + 0.5) * (1.0 / 9.0))
    place = lax.broadcasted_iota(jnp.int32, (slab, 128), 0)
    xs_ref[0:slab] = jnp.zeros((slab, 1152), jnp.bfloat16)
    xs_ref[5 * slab : 6 * slab] = jnp.zeros((slab, 1152), jnp.bfloat16)
    f_ref[...] = jnp.zeros_like(f_ref)
    now = x_ref[...].astype(jnp.float32)
    f_ref[2, pad : pad + rows] = now
    back1 = jnp.where(frame < 0.5, now, f_ref[2, pad - 1 : pad - 1 + rows])
    f_ref[1, pad : pad + rows] = back1
    f_ref[0, pad : pad + rows] = jnp.where(
        frame < 1.5, back1, f_ref[2, pad - 2 : pad - 2 + rows]
    )
    for h in range(4):
        for dw in range(3):
            for kd in range(3):
                start = pad + h * slab + (dw - 1) * 36
                piece = f_ref[kd, start : start + slab]
                if dw == 0:
                    piece = jnp.where(place < 36, 0.0, piece)
                if dw == 2:
                    piece = jnp.where(place >= slab - 36, 0.0, piece)
                col = dw * 384 + kd * 128
                xs_ref[(h + 1) * slab : (h + 2) * slab, col : col + 128] = piece.astype(
                    jnp.bfloat16
                )


def combine_weights(w_ref, wz_ref):
    chans = 128
    for kd in range(3):
        tap = {}
        for kh in range(3):
            for kw in range(3):
                piece = w_ref[:, 9 * kd + 3 * kh + kw]
                tap[kh, kw] = piece.reshape(chans, chans).astype(jnp.float32)
        for ph in range(2):
            for a in range(2):
                line = [sum(tap[kh, kw] for kh in TAPS[ph, a]) for kw in range(3)]
                for pw in range(2):
                    for b in range(2):
                        both = sum(line[kw] for kw in TAPS[pw, b])
                        row = (b + pw) * 384 + kd * 128
                        col = (2 * ph + pw) * 128
                        wz_ref[a + ph, row : row + 128, col : col + 128] = both.astype(
                            jnp.bfloat16
                        )


def products(count, xs_ref, cot_ref, bias_ref, wz_ref, g_ref):
    slab = xs_ref.shape[0] // 6
    rows = 4 * slab
    row = lax.broadcasted_iota(jnp.int32, (rows, 128), 0).astype(jnp.float32)
    place = row - 36.0 * jnp.floor((row + 0.5) * (1.0 / 36.0))
    live = place < 9.0 * count.astype(jnp.float32)
    cols = ((0, 256), (0, 512), (256, 256))

    def window(dh):
        return xs_ref[dh * slab : dh * slab + rows, :]

    mid = jnp.dot(window(1), wz_ref[1], preferred_element_type=jnp.float32)
    top = jnp.dot(window(0), wz_ref[0, :, 0:256], preferred_element_type=jnp.float32)
    low = jnp.dot(window(2), wz_ref[2, :, 256:512], preferred_element_type=jnp.float32)
    parts = []
    total_b = jnp.zeros((1, 128), jnp.float32)
    for p in range(4):
        side = (top if p < 2 else low)[:, (p % 2) * 128 : (p % 2) * 128 + 128]
        z = mid[:, p * 128 : p * 128 + 128] + side + bias_ref[...]
        sig = jax.nn.sigmoid(z)
        dz = cot_ref[p].astype(jnp.float32) * sig * (1.0 + z * (1.0 - sig))
        dz = jnp.where(live, dz, 0.0).astype(jnp.bfloat16)
        total_b += jnp.sum(dz.astype(jnp.float32), axis=0, keepdims=True)
        parts.append(dz)
    dz = jnp.concatenate(parts, axis=1)
    for dh in range(3):
        start, width = cols[dh]
        g_ref[dh, :, start : start + width] = lax.dot_general(
            window(dh),
            dz[:, start : start + width],
            (((0,), (0,)), ((), ())),
            preferred_element_type=jnp.float32,
        )
    return total_b


def tap_gradient(g_ref, k, base=0, size=128):
    kd, kh, kw = k // 9, k // 3 % 3, k % 3
    total = None
    for ph in range(2):
        for pw in range(2):
            row = (OFFSET[pw][kw] + pw) * 384 + kd * 128
            col = (2 * ph + pw) * 128
            term = g_ref[
                OFFSET[ph][kh] + ph, pl.ds(base + row, size), col : col + 128
            ]
            total = term if total is None else total + term
    return total


WORK = [
    pltpu.VMEM((3, 656, 128), jnp.float32),
    pltpu.VMEM((864, 1152), jnp.bfloat16),
    pltpu.VMEM((3, 1152, 512), jnp.bfloat16),
    pltpu.VMEM((3, 1152, 512), jnp.float32),
]


def terms_kernel(
    count_ref, w_ref, x_ref, cot_ref, bias_ref, out_ref, f_ref, xs_ref, wz_ref, g_ref
):
    build_windows(x_ref, f_ref, xs_ref)
    wz_ref[...] = jnp.zeros_like(wz_ref)
    combine_weights(w_ref, wz_ref)
    total_b = products(count_ref[0], xs_ref, cot_ref, bias_ref, wz_ref, g_ref)
    for k in range(27):
        out_ref[:, k] = tap_gradient(g_ref, k).reshape(8, 16, 128)
    out_ref[:, 27] = jnp.broadcast_to(total_b.reshape(1, 1, 128), (8, 16, 128))


def terms(count, w, x, cot, bias):
    return pl.pallas_call(
        terms_kernel,
        out_shape=jax.ShapeDtypeStruct((8, 28, 16, 128), jnp.float32),
        in_specs=[pl.BlockSpec(memory_space=pltpu.SMEM)]
        + [pl.BlockSpec(memory_space=pltpu.VMEM)] * 4,
        out_specs=pl.BlockSpec(memory_space=pltpu.VMEM),
        scratch_shapes=WORK,
        compiler_params=pltpu.CompilerParams(vmem_limit_bytes=48 * 2**20),
    )(count, w, x, cot, bias)


def xor(value, mask):
    if mask == 1:
        return value + 1 - 2 * (value % 2)
    if mask == 2:
        return (value + 2) % 4
    return 3 - value


def lay_out_tiles(x_raw, f_ref, xs_ref, xt_ref):
    pad = 8
    rows = 576
    full = x_raw[...].astype(jnp.float32)
    for tf in range(36):
        for h in range(4):
            at = pad + h * 144 + tf * 4
            f_ref[2, at : at + 4] = full[tf * 16 + h * 4 : tf * 16 + h * 4 + 4]
    row = lax.broadcasted_iota(jnp.int32, (144, 128), 0)
    w = row % 4
    frame = (row // 4) % 9
    for h in range(4):
        at = pad + h * 144
        now = f_ref[2, at : at + 144]
        back1 = jnp.where(frame < 1, now, f_ref[2, at - 4 : at + 140])
        back2 = jnp.where(frame < 2, back1, f_ref[2, at - 8 : at + 136])
        f_ref[1, at : at + 144] = back1
        f_ref[0, at : at + 144] = back2
    for kd in range(3):
        for h in range(4):
            at = pad + h * 144
            lines = slice(h * 144, h * 144 + 144)
            left = jnp.where(w == 0, 0.0, f_ref[kd, at - 1 : at + 143])
            here = f_ref[kd, at : at + 144]
            right = jnp.where(w == 3, 0.0, f_ref[kd, at + 1 : at + 145])
            left, here, right = (
                piece.astype(jnp.bfloat16) for piece in (left, here, right)
            )
            col = kd * 256
            xs_ref[0, lines, col : col + 128] = left
            xs_ref[0, lines, col + 128 : col + 256] = here
            xs_ref[1, lines, col : col + 128] = here
            xs_ref[1, lines, col + 128 : col + 256] = right
    for kd in range(3):
        for pw in range(2):
            for b in range(2):
                col = kd * 256 + b * 128
                if (pw, b) == (1, 0):
                    continue
                block = xs_ref[pw, :, col : col + 128].astype(jnp.float32).T
                block = block.astype(jnp.bfloat16)
                for part in range(4):
                    piece = block[part * 32 : part * 32 + 32]
                    at = kd * 64 + b * 32
                    xt_ref[part, pw, at : at + 32, :] = piece
                    if (pw, b) == (0, 1):
                        xt_ref[part, 1, kd * 64 : kd * 64 + 32, :] = piece


def lay_out_cotangent(cot_raw, cf_ref, cp_ref):
    for tf in range(36):
        full = cot_raw[tf * 64 : tf * 64 + 64].astype(jnp.float32)
        for line in range(8):
            cf_ref[line, tf * 8 : tf * 8 + 8] = full[line * 8 : line * 8 + 8]
    for h in range(4):
        for ph in range(2):
            for pw in range(2):
                cp_ref[2 * ph + pw, h * 144 : h * 144 + 144] = cf_ref[
                    2 * h + ph, pl.ds(pw, 144, 2), :
                ]


def spread_rows(w_ref, d, wf_ref):
    for q in range(4):
        at = (7 * q - q // 3) * 16
        wf_ref[at : at + 112] = w_ref[d, q].astype(jnp.float32)


def combine_shard(wf_ref, d, wz_ref):
    for kd in range(3):
        tap = {}
        for kh in range(3):
            for kw in range(3):
                tap[kh, kw] = wf_ref[pl.ds(9 * kd + 3 * kh + kw, 16, 27), :]
        for ph in range(2):
            for a in range(2):
                line = [sum(tap[kh, kw] for kh in TAPS[ph, a]) for kw in range(3)]
                for pw in range(2):
                    for b in range(2):
                        both = sum(line[kw] for kw in TAPS[pw, b])
                        row = pl.multiple_of(kd * 256 + b * 128 + d * 16, 16)
                        col = (2 * ph + a) * 128
                        wz_ref[pw, pl.ds(row, 16), col : col + 128] = both.astype(
                            jnp.bfloat16
                        )


def forward(count, xs_ref, wz_ref, y_ref, cp_ref, bias_ref, dz_ref):
    f32 = jnp.float32
    place = lax.broadcasted_iota(jnp.int32, (144, 128), 0)
    live = place < 36 * count
    total_b = jnp.zeros((1, 128), f32)
    for pw in range(2):
        y_ref[pw] = jnp.dot(xs_ref[pw], wz_ref[pw], preferred_element_type=f32)
    for pw in range(2):
        for ph in range(2):
            for h in range(4):
                lines = slice(h * 144, h * 144 + 144)
                col = ph * 256
                z = bias_ref[...]
                for a in range(2):
                    s = h + a + ph - 1
                    if 0 <= s < 4:
                        z = z + y_ref[
                            pw,
                            s * 144 : s * 144 + 144,
                            col + a * 128 : col + a * 128 + 128,
                        ]
                sig = 0.5 + 0.5 * jnp.tanh(0.5 * z)
                dz = cp_ref[2 * ph + pw, lines] * sig * (1.0 + z * (1.0 - sig))
                dz = jnp.where(live, dz, 0.0).astype(jnp.bfloat16)
                total_b += jnp.sum(dz.astype(f32), axis=0, keepdims=True)
                for a in range(2):
                    s = h + a + ph - 1
                    if 0 <= s < 4:
                        dz_ref[
                            pw,
                            s * 144 : s * 144 + 144,
                            col + a * 128 : col + a * 128 + 128,
                        ] = dz
    return total_b


def clear_edges(dz_ref):
    zero = jnp.zeros((144, 128), jnp.bfloat16)
    for pw in range(2):
        dz_ref[pw, 432:576, 0:128] = zero
        dz_ref[pw, 0:144, 384:512] = zero


def backward(xt_ref, part, dz_ref, g_ref, k):
    for pw in range(2):
        g_ref[k, pw] = jnp.dot(
            xt_ref[part, pw], dz_ref[pw], preferred_element_type=jnp.float32
        )


def tap_sums(g_ref, k, base, store):
    for kd in range(3):
        line = {}
        for pw in range(2):
            for b in range(2):
                row = pl.multiple_of(kd * 64 + b * 32 + base, 16)
                part = [
                    g_ref[k, pw, pl.ds(row, 16), c * 128 : c * 128 + 128]
                    for c in range(4)
                ]
                for kh in range(3):
                    line[pw, b, kh] = part[OFFSET[0][kh]] + part[2 + OFFSET[1][kh]]
        for kh in range(3):
            for kw in range(3):
                store(
                    9 * kd + 3 * kh + kw,
                    line[0, OFFSET[0][kw], kh] + line[1, OFFSET[1][kw], kh],
                )


def whole_kernel(
    scale, counts_any, w_any, x_any, cot_any, bias_any, o_any, b_ref,
    counts_ref, w_raw, w_pair, x_raw, cot_raw, bias_ref,
    wf_ref, f_ref, cf_ref, cp_ref, xs_ref, xt_ref, wz_ref, y_ref, dz_ref, g_ref,
    w_all, parts, s1, r1, s2, r2, keep, s3, r3, last, sb, rb,
    fetch, sw3, rw3, sw1, rw1, sw2, rw2, ss1, rs1, ss2, rs2, ss3, rs3, ss4, rs4, ssb, rsb,
):
    grp = lax.axis_index("grp")
    dev = lax.axis_index("dev")
    depth = dev // 2
    core = dev % 2
    f32, bf16 = jnp.float32, jnp.bfloat16
    masks = (3, 2, 1)
    pair = {"dev": depth * 2 + (1 - core)}
    across = [{"grp": xor(grp, m)} for m in masks]
    along = [{"dev": xor(depth, m) * 2 + core} for m in masks]

    fetches = []
    for i, (src, dst) in enumerate(
        (
            (w_any, w_raw),
            (cot_any, cot_raw),
            (x_any, x_raw),
            (bias_any, bias_ref),
            (counts_any, counts_ref),
        )
    ):
        fetches.append(pltpu.make_async_copy(src, dst, fetch.at[i]))
        fetches[i].start()

    barrier = pltpu.get_barrier_semaphore()
    for peer in [pair] + across + along:
        pl.semaphore_signal(barrier, inc=1, device_id=peer, device_id_type=MESH)

    def send(src, dst, ssem, rsem, peer):
        copy = pltpu.make_async_remote_copy(
            src_ref=src, dst_ref=dst, send_sem=ssem, recv_sem=rsem,
            device_id=peer, device_id_type=MESH,
        )
        copy.start()
        return copy

    pl.semaphore_wait(barrier, 7)

    fetches[0].wait()
    quarter = w_raw.at[pl.ds(pl.multiple_of((7 * grp - grp // 3) * 16, 16), 112)]
    out = [
        send(quarter, w_all.at[dev, grp], sw1.at[k], rw1.at[k], along[k])
        for k in range(3)
    ]
    swap = [send(w_raw, w_pair, sw2.at[3], rw2.at[3], pair)]
    clear_edges(dz_ref)
    zero = jnp.zeros((16, 128), bf16)
    for k in range(4):
        s1[k, 27] = zero
        parts[k, 27] = jnp.zeros((16, 128), f32)
    wf_ref[0] = w_raw[...].astype(f32)
    combine_shard(wf_ref.at[0], dev, wz_ref)
    fetches[1].wait()
    lay_out_cotangent(cot_raw, cf_ref, cp_ref)
    spread = {}
    for k in (2, 1, 0):
        out[k].wait_recv()
        block = w_all.at[xor(depth, masks[k]) * 2 + core, grp]
        for j in range(3):
            spread[k, j] = send(block, block, sw3.at[k, j], rw3.at[k, j], across[j])
    fetches[2].wait()
    lay_out_tiles(x_raw, f_ref, xs_ref, xt_ref)
    swap[0].wait_recv()
    wf_ref[1] = w_pair[...].astype(f32)
    combine_shard(wf_ref.at[1], depth * 2 + 1 - core, wz_ref)
    for k in (2, 1, 0):
        for j in range(3):
            spread[k, j].wait_recv()
        block = w_all.at[xor(depth, masks[k]) * 2 + core]
        swap.append(send(block, block, sw2.at[k], rw2.at[k], pair))
        spread_rows(w_all, xor(depth, masks[k]) * 2 + core, wf_ref.at[0])
        combine_shard(wf_ref.at[0], xor(depth, masks[k]) * 2 + core, wz_ref)
    for i, k in enumerate((2, 1, 0)):
        swap[1 + i].wait_recv()
        spread_rows(w_all, xor(depth, masks[k]) * 2 + 1 - core, wf_ref.at[1])
        combine_shard(wf_ref.at[1], xor(depth, masks[k]) * 2 + 1 - core, wz_ref)
    fetches[3].wait()
    fetches[4].wait()
    total_b = forward(
        counts_ref[grp * 8 + dev], xs_ref, wz_ref, y_ref, cp_ref, bias_ref, dz_ref
    )

    sb[0] = jnp.broadcast_to(total_b, (8, 128))
    bias_start = send(sb.at[0], rb.at[0], ssb.at[0], rsb.at[0], pair)
    for copy in out + list(spread.values()) + swap:
        copy.wait_send()

    def reduce_all(early):
        first, second, third = {}, {}, {}
        ahead = (3, 2, 1, 0)

        def work(k):
            backward(xt_ref, xor(depth, ahead[k]) if ahead[k] else depth, dz_ref, g_ref, k)

        def give(k):
            def to_pair(tap, value):
                s1[k, tap] = value.astype(bf16)

            tap_sums(g_ref, k, 16 if early else 0, to_pair)
            first[k] = send(s1.at[k], r1.at[k], ss1.at[k], rs1.at[k], pair)

        def own(k):
            def to_self(tap, value):
                parts[k, tap] = value

            tap_sums(g_ref, k, 0 if early else 16, to_self)

        def start_second(k):
            arrived = pltpu.make_async_remote_copy(
                src_ref=s1.at[k], dst_ref=r1.at[k], send_sem=ss1.at[k], recv_sem=rs1.at[k],
                device_id=pair, device_id_type=MESH,
            )
            arrived.wait_recv()
            for j in range(4):
                owner = xor(grp, masks[j]) if j < 3 else grp
                taps = pl.ds(owner * 7, 7)
                total = parts[k, taps] + r1[k, taps].astype(f32)
                if j < 3:
                    s2[k, j] = total.astype(bf16)
                    second[k, j] = send(
                        s2.at[k, j], r2.at[k, j], ss2.at[k, j], rs2.at[k, j], across[j]
                    )
                else:
                    keep[k] = total

        def start_third(k):
            total = keep[k]
            for j in range(3):
                second[k, j].wait_recv()
                total += r2[k, j].astype(f32)
            if k < 3:
                s3[k] = total.astype(bf16)
                third[k] = send(s3.at[k], r3.at[k], ss3.at[k], rs3.at[k], along[k])
            else:
                keep[k] = total

        bias_copies = []

        def bias_across():
            bias_start.wait_recv()
            sb[1] = sb[0] + rb[0]
            for k in range(3):
                bias_copies.append(
                    send(sb.at[1], rb.at[1 + k], ssb.at[1 + k], rsb.at[1 + k], across[k])
                )

        def bias_along():
            for k in range(3):
                bias_copies[k].wait_recv()
            sb[2] = (sb[1] + rb[3]) + (rb[2] + rb[1])
            for k in range(3):
                bias_copies.append(
                    send(sb.at[2], rb.at[4 + k], ssb.at[4 + k], rsb.at[4 + k], along[k])
                )

        if early:
            work(0)
            own(0)
            work(1)
            own(1)
            start_second(0)
            work(2)
            own(2)
            start_second(1)
            work(3)
            own(3)
            start_second(2)
            give(0)
            start_second(3)
            give(1)
            give(2)
            give(3)
            bias_across()
        else:
            for k in range(4):
                work(k)
                give(k)
            bias_across()
            for k in range(4):
                own(k)
                start_second(k)
        start_third(0)
        start_third(1)
        start_third(2)
        bias_along()
        start_third(3)
        total = keep[3]
        for k in (2, 1, 0):
            third[k].wait_recv()
            total += r3[k].astype(f32)
        last[...] = (total * scale).astype(bf16)
        fourth = [
            send(last, o_any.at[grp], ss4.at[k], rs4.at[k], across[k]) for k in range(3)
        ]
        mine = pltpu.make_async_copy(last, o_any.at[grp], fetch.at[5])
        mine.start()
        for k in range(3):
            bias_copies[3 + k].wait_recv()
        whole_b = (((sb[2] + rb[6]) + (rb[5] + rb[4])) * scale)[0:1]
        share = jnp.zeros((1, 16), f32)
        for d in range(8):
            share = jnp.where(dev == d, whole_b[:, d * 16 : d * 16 + 16], share)
        b_ref[...] = share
        for copy in list(first.values()) + list(second.values()) + list(third.values()):
            copy.wait_send()
        for copy in [bias_start] + bias_copies + fourth:
            copy.wait_send()
        mine.wait()
        for k in (2, 1, 0):
            fourth[k].wait_recv()

    @pl.when(core == 0)
    def _():
        reduce_all(True)

    @pl.when(core == 1)
    def _():
        reduce_all(False)


def whole(counts, w, x, cot, bias, scale):
    bf16, f32 = jnp.bfloat16, jnp.float32
    sem = pltpu.SemaphoreType.DMA
    vmem = pltpu.VMEM
    return pl.pallas_call(
        functools.partial(whole_kernel, scale),
        out_shape=(
            jax.ShapeDtypeStruct((4, 7, 16, 128), bf16),
            jax.ShapeDtypeStruct((1, 16), f32),
        ),
        in_specs=[pl.BlockSpec(memory_space=pltpu.HBM)] * 5,
        out_specs=[
            pl.BlockSpec(memory_space=pltpu.HBM),
            pl.BlockSpec(memory_space=pltpu.VMEM),
        ],
        scratch_shapes=[
            pltpu.SMEM((32,), jnp.int32),
            vmem((432, 128), bf16),
            vmem((432, 128), bf16),
            vmem((576, 128), bf16),
            vmem((2304, 128), bf16),
            vmem((1, 128), f32),
            vmem((2, 432, 128), f32),
            vmem((3, 592, 128), f32),
            vmem((8, 288, 128), f32),
            vmem((4, 576, 128), f32),
            vmem((2, 576, 768), bf16),
            vmem((4, 2, 192, 576), bf16),
            vmem((2, 768, 512), bf16),
            vmem((2, 576, 512), f32),
            vmem((2, 576, 512), bf16),
            vmem((4, 2, 192, 512), f32),
            vmem((8, 4, 112, 128), bf16),
            vmem((4, 28, 16, 128), f32),
            vmem((4, 28, 16, 128), bf16),
            vmem((4, 28, 16, 128), bf16),
            vmem((4, 3, 7, 16, 128), bf16),
            vmem((4, 3, 7, 16, 128), bf16),
            vmem((4, 7, 16, 128), f32),
            vmem((3, 7, 16, 128), bf16),
            vmem((3, 7, 16, 128), bf16),
            vmem((7, 16, 128), bf16),
            vmem((3, 8, 128), f32),
            vmem((7, 8, 128), f32),
            sem((6,)), sem((3, 3)), sem((3, 3)),
            sem((3,)), sem((3,)), sem((4,)), sem((4,)),
            sem((4,)), sem((4,)), sem((4, 3)), sem((4, 3)),
            sem((3,)), sem((3,)), sem((3,)), sem((3,)),
            sem((7,)), sem((7,)),
        ],
        compiler_params=pltpu.CompilerParams(
            collective_id=1, has_side_effects=True, vmem_limit_bytes=60 * 2**20
        ),
    )(counts, w, x, cot, bias)


def sort_rows_kernel(w_ref, b_ref, o_any, p_any, rows_ref, sems):
    bias = pltpu.make_async_copy(b_ref, p_any, sems.at[1])
    bias.start()
    for k in range(27):
        rows_ref[pl.ds(k, 16, 27), :] = w_ref[k // 7, k % 7].astype(jnp.float32)
    copy = pltpu.make_async_copy(rows_ref, o_any, sems.at[0])
    copy.start()
    bias.wait()
    copy.wait()


def sort_rows(part_w, part_b):
    f32 = jnp.float32
    return pl.pallas_call(
        sort_rows_kernel,
        out_shape=(
            jax.ShapeDtypeStruct((432, 128), f32),
            jax.ShapeDtypeStruct(part_b.shape, f32),
        ),
        in_specs=[pl.BlockSpec(memory_space=pltpu.VMEM)] * 2,
        out_specs=[pl.BlockSpec(memory_space=pltpu.HBM)] * 2,
        scratch_shapes=[pltpu.VMEM((432, 128), f32), pltpu.SemaphoreType.DMA((2,))],
    )(part_w, part_b)


def body(tiles, cotangent, weight, bias, counts):
    num_dev = lax.axis_size("dev")
    num_grp = lax.axis_size("grp")
    cap, frames, hl, wl, cin = tiles.shape
    cout = weight.shape[1]
    my_dev = lax.axis_index("dev")
    my_grp = lax.axis_index("grp")
    scale = 1.0 / math.sqrt(cap * num_dev * num_grp * frames * 4 * hl * wl)
    bias = bias.reshape(1, cout)
    if (num_grp, num_dev) == (4, 8):
        x = tiles.reshape(cap * frames * hl * wl, cin)
        cot = cotangent.reshape(cap * frames * 4 * hl * wl, cout)
        part_w, part_b = sort_rows(*whole(counts, weight, x, cot, bias, scale))
        return part_w, part_b.reshape(cout // num_dev)

    mine = weight.reshape(cin // num_dev, 27, cout).transpose(1, 0, 2)
    x = tiles.transpose(2, 3, 0, 1, 4).reshape(hl * wl * cap * frames, cin)
    cot = cotangent.reshape(cap, frames, hl, 2, wl, 2, cout).transpose(3, 5, 2, 4, 0, 1, 6)
    cot = cot.reshape(4, hl * wl * cap * frames, cout)
    share = cout // num_dev
    gathered = lax.all_gather(mine, "dev", axis=0, tiled=False)
    if num_dev != 8:
        gathered = gathered.transpose(1, 0, 2, 3).reshape(27, 8, 16, cout)
        gathered = gathered.transpose(1, 0, 2, 3)
    count = lax.dynamic_slice_in_dim(counts, my_grp * num_dev + my_dev, 1)
    parts = terms(count, gathered, x, cot, bias)
    flat = parts[:, :27].transpose(0, 2, 1, 3).reshape(cin * 27, cout)
    part_w = lax.psum_scatter(flat, "dev", scatter_dimension=0, tiled=True)
    part_w = lax.psum(part_w, "grp")
    total_b = lax.psum(parts[0, 27, 0], ("grp", "dev"))
    part_b = lax.dynamic_slice_in_dim(total_b, my_dev * share, share, 0)
    return part_w * scale, part_b * scale


def solution(mesh):
    return jax.shard_map(
        body,
        mesh=mesh,
        in_specs=(
            P(("grp", "dev"), None, None, None, None),
            P(("grp", "dev"), None, None, None, None),
            P("dev", None),
            P(),
            P(),
        ),
        out_specs=(P("dev", None), P("dev")),
        check_vma=False,
    )
```

```python
import functools
import math

import jax
import jax.numpy as jnp
from jax import lax
from jax.experimental import pallas as pl
from jax.experimental.pallas import tpu as pltpu
from jax.sharding import PartitionSpec as P

MESH = pl.DeviceIdType.MESH
TAPS = {(0, 0): (0,), (0, 1): (1, 2), (1, 0): (0, 1), (1, 1): (2,)}
OFFSET = ((0, 1, 1), (0, 0, 1))


def build_windows(x_ref, f_ref, xs_ref):
    rows = x_ref.shape[0]
    slab = rows // 4
    pad = 40
    row = lax.broadcasted_iota(jnp.int32, (rows, 128), 0).astype(jnp.float32)
    frame = row - 9.0 * jnp.floor((row + 0.5) * (1.0 / 9.0))
    place = lax.broadcasted_iota(jnp.int32, (slab, 128), 0)
    xs_ref[0:slab] = jnp.zeros((slab, 1152), jnp.bfloat16)
    xs_ref[5 * slab : 6 * slab] = jnp.zeros((slab, 1152), jnp.bfloat16)
    f_ref[...] = jnp.zeros_like(f_ref)
    now = x_ref[...].astype(jnp.float32)
    f_ref[2, pad : pad + rows] = now
    back1 = jnp.where(frame < 0.5, now, f_ref[2, pad - 1 : pad - 1 + rows])
    f_ref[1, pad : pad + rows] = back1
    f_ref[0, pad : pad + rows] = jnp.where(
        frame < 1.5, back1, f_ref[2, pad - 2 : pad - 2 + rows]
    )
    for h in range(4):
        for dw in range(3):
            for kd in range(3):
                start = pad + h * slab + (dw - 1) * 36
                piece = f_ref[kd, start : start + slab]
                if dw == 0:
                    piece = jnp.where(place < 36, 0.0, piece)
                if dw == 2:
                    piece = jnp.where(place >= slab - 36, 0.0, piece)
                col = dw * 384 + kd * 128
                xs_ref[(h + 1) * slab : (h + 2) * slab, col : col + 128] = piece.astype(
                    jnp.bfloat16
                )


def combine_weights(w_ref, wz_ref):
    chans = 128
    for kd in range(3):
        tap = {}
        for kh in range(3):
            for kw in range(3):
                piece = w_ref[:, 9 * kd + 3 * kh + kw]
                tap[kh, kw] = piece.reshape(chans, chans).astype(jnp.float32)
        for ph in range(2):
            for a in range(2):
                line = [sum(tap[kh, kw] for kh in TAPS[ph, a]) for kw in range(3)]
                for pw in range(2):
                    for b in range(2):
                        both = sum(line[kw] for kw in TAPS[pw, b])
                        row = (b + pw) * 384 + kd * 128
                        col = (2 * ph + pw) * 128
                        wz_ref[a + ph, row : row + 128, col : col + 128] = both.astype(
                            jnp.bfloat16
                        )


def products(count, xs_ref, cot_ref, bias_ref, wz_ref, g_ref):
    slab = xs_ref.shape[0] // 6
    rows = 4 * slab
    row = lax.broadcasted_iota(jnp.int32, (rows, 128), 0).astype(jnp.float32)
    place = row - 36.0 * jnp.floor((row + 0.5) * (1.0 / 36.0))
    live = place < 9.0 * count.astype(jnp.float32)
    cols = ((0, 256), (0, 512), (256, 256))

    def window(dh):
        return xs_ref[dh * slab : dh * slab + rows, :]

    mid = jnp.dot(window(1), wz_ref[1], preferred_element_type=jnp.float32)
    top = jnp.dot(window(0), wz_ref[0, :, 0:256], preferred_element_type=jnp.float32)
    low = jnp.dot(window(2), wz_ref[2, :, 256:512], preferred_element_type=jnp.float32)
    parts = []
    total_b = jnp.zeros((1, 128), jnp.float32)
    for p in range(4):
        side = (top if p < 2 else low)[:, (p % 2) * 128 : (p % 2) * 128 + 128]
        z = mid[:, p * 128 : p * 128 + 128] + side + bias_ref[...]
        sig = jax.nn.sigmoid(z)
        dz = cot_ref[p].astype(jnp.float32) * sig * (1.0 + z * (1.0 - sig))
        dz = jnp.where(live, dz, 0.0).astype(jnp.bfloat16)
        total_b += jnp.sum(dz.astype(jnp.float32), axis=0, keepdims=True)
        parts.append(dz)
    dz = jnp.concatenate(parts, axis=1)
    for dh in range(3):
        start, width = cols[dh]
        g_ref[dh, :, start : start + width] = lax.dot_general(
            window(dh),
            dz[:, start : start + width],
            (((0,), (0,)), ((), ())),
            preferred_element_type=jnp.float32,
        )
    return total_b


def tap_gradient(g_ref, k, base=0, size=128):
    kd, kh, kw = k // 9, k // 3 % 3, k % 3
    total = None
    for ph in range(2):
        for pw in range(2):
            row = (OFFSET[pw][kw] + pw) * 384 + kd * 128
            col = (2 * ph + pw) * 128
            term = g_ref[
                OFFSET[ph][kh] + ph, pl.ds(base + row, size), col : col + 128
            ]
            total = term if total is None else total + term
    return total


WORK = [
    pltpu.VMEM((3, 656, 128), jnp.float32),
    pltpu.VMEM((864, 1152), jnp.bfloat16),
    pltpu.VMEM((3, 1152, 512), jnp.bfloat16),
    pltpu.VMEM((3, 1152, 512), jnp.float32),
]


def terms_kernel(
    count_ref, w_ref, x_ref, cot_ref, bias_ref, out_ref, f_ref, xs_ref, wz_ref, g_ref
):
    build_windows(x_ref, f_ref, xs_ref)
    wz_ref[...] = jnp.zeros_like(wz_ref)
    combine_weights(w_ref, wz_ref)
    total_b = products(count_ref[0], xs_ref, cot_ref, bias_ref, wz_ref, g_ref)
    for k in range(27):
        out_ref[:, k] = tap_gradient(g_ref, k).reshape(8, 16, 128)
    out_ref[:, 27] = jnp.broadcast_to(total_b.reshape(1, 1, 128), (8, 16, 128))


def terms(count, w, x, cot, bias):
    return pl.pallas_call(
        terms_kernel,
        out_shape=jax.ShapeDtypeStruct((8, 28, 16, 128), jnp.float32),
        in_specs=[pl.BlockSpec(memory_space=pltpu.SMEM)]
        + [pl.BlockSpec(memory_space=pltpu.VMEM)] * 4,
        out_specs=pl.BlockSpec(memory_space=pltpu.VMEM),
        scratch_shapes=WORK,
        compiler_params=pltpu.CompilerParams(vmem_limit_bytes=48 * 2**20),
    )(count, w, x, cot, bias)


def xor(value, mask):
    if mask == 1:
        return value + 1 - 2 * (value % 2)
    if mask == 2:
        return (value + 2) % 4
    return 3 - value


def lay_out_tiles(x_raw, f_ref, xs_ref, xt_ref):
    pad = 8
    rows = 576
    full = x_raw[...].astype(jnp.float32)
    for tf in range(36):
        for h in range(4):
            at = pad + h * 144 + tf * 4
            f_ref[2, at : at + 4] = full[tf * 16 + h * 4 : tf * 16 + h * 4 + 4]
    row = lax.broadcasted_iota(jnp.int32, (144, 128), 0)
    w = row % 4
    frame = (row // 4) % 9
    for h in range(4):
        at = pad + h * 144
        now = f_ref[2, at : at + 144]
        back1 = jnp.where(frame < 1, now, f_ref[2, at - 4 : at + 140])
        back2 = jnp.where(frame < 2, back1, f_ref[2, at - 8 : at + 136])
        f_ref[1, at : at + 144] = back1
        f_ref[0, at : at + 144] = back2
    for kd in range(3):
        for h in range(4):
            at = pad + h * 144
            lines = slice(h * 144, h * 144 + 144)
            left = jnp.where(w == 0, 0.0, f_ref[kd, at - 1 : at + 143])
            here = f_ref[kd, at : at + 144]
            right = jnp.where(w == 3, 0.0, f_ref[kd, at + 1 : at + 145])
            left, here, right = (
                piece.astype(jnp.bfloat16) for piece in (left, here, right)
            )
            col = kd * 256
            xs_ref[0, lines, col : col + 128] = left
            xs_ref[0, lines, col + 128 : col + 256] = here
            xs_ref[1, lines, col : col + 128] = here
            xs_ref[1, lines, col + 128 : col + 256] = right
    for kd in range(3):
        for pw in range(2):
            for b in range(2):
                col = kd * 256 + b * 128
                if (pw, b) == (1, 0):
                    continue
                block = xs_ref[pw, :, col : col + 128].astype(jnp.float32).T
                block = block.astype(jnp.bfloat16)
                for part in range(4):
                    piece = block[part * 32 : part * 32 + 32]
                    at = kd * 64 + b * 32
                    xt_ref[part, pw, at : at + 32, :] = piece
                    if (pw, b) == (0, 1):
                        xt_ref[part, 1, kd * 64 : kd * 64 + 32, :] = piece


def lay_out_cotangent(cot_raw, cf_ref, cp_ref):
    for tf in range(36):
        full = cot_raw[tf * 64 : tf * 64 + 64].astype(jnp.float32)
        for line in range(8):
            cf_ref[line, tf * 8 : tf * 8 + 8] = full[line * 8 : line * 8 + 8]
    for h in range(4):
        for ph in range(2):
            for pw in range(2):
                cp_ref[2 * ph + pw, h * 144 : h * 144 + 144] = cf_ref[
                    2 * h + ph, pl.ds(pw, 144, 2), :
                ]


def spread_rows(w_ref, d, wf_ref):
    for q in range(4):
        at = (7 * q - q // 3) * 16
        wf_ref[at : at + 112] = w_ref[d, q].astype(jnp.float32)


def combine_shard(wf_ref, d, wz_ref):
    for kd in range(3):
        tap = {}
        for kh in range(3):
            for kw in range(3):
                tap[kh, kw] = wf_ref[pl.ds(9 * kd + 3 * kh + kw, 16, 27), :]
        for ph in range(2):
            for a in range(2):
                line = [sum(tap[kh, kw] for kh in TAPS[ph, a]) for kw in range(3)]
                for pw in range(2):
                    for b in range(2):
                        both = sum(line[kw] for kw in TAPS[pw, b])
                        row = pl.multiple_of(kd * 256 + b * 128 + d * 16, 16)
                        col = (2 * ph + a) * 128
                        wz_ref[pw, pl.ds(row, 16), col : col + 128] = both.astype(
                            jnp.bfloat16
                        )


def forward(count, xs_ref, wz_ref, y_ref, cp_ref, bias_ref, dz_ref):
    f32 = jnp.float32
    place = lax.broadcasted_iota(jnp.int32, (144, 128), 0)
    live = place < 36 * count
    units = [(pw, ph) for pw in range(2) for ph in range(2)]
    totals = []

    def multiply(pw, ph):
        y_ref[2 * pw + ph] = jnp.dot(
            xs_ref[pw],
            wz_ref[pw, :, ph * 256 : ph * 256 + 256],
            preferred_element_type=f32,
        )

    def finish(pw, ph):
        for h in range(4):
            z = bias_ref[...]
            for a in range(2):
                s = h + a + ph - 1
                if 0 <= s < 4:
                    z = z + y_ref[
                        2 * pw + ph, s * 144 : s * 144 + 144, a * 128 : a * 128 + 128
                    ]
            sig = 0.5 + 0.5 * jnp.tanh(0.5 * z)
            lines = slice(h * 144, h * 144 + 144)
            dz = cp_ref[2 * ph + pw, lines] * sig * (1.0 + z * (1.0 - sig))
            dz = jnp.where(live, dz, 0.0).astype(jnp.bfloat16)
            totals.append(jnp.sum(dz.astype(f32), axis=0, keepdims=True))
            for a in range(2):
                s = h + a + ph - 1
                if 0 <= s < 4:
                    col = ph * 256 + a * 128
                    dz_ref[pw, s * 144 : s * 144 + 144, col : col + 128] = dz

    multiply(*units[0])
    for step in range(4):
        if step < 3:
            multiply(*units[step + 1])
        finish(*units[step])
    return sum(totals)


def clear_edges(dz_ref):
    zero = jnp.zeros((144, 128), jnp.bfloat16)
    for pw in range(2):
        dz_ref[pw, 432:576, 0:128] = zero
        dz_ref[pw, 0:144, 384:512] = zero


def backward(xt_ref, part, dz_ref, g_ref, k):
    for pw in range(2):
        g_ref[k, pw] = jnp.dot(
            xt_ref[part, pw], dz_ref[pw], preferred_element_type=jnp.float32
        )


def tap_sums(g_ref, k, base, store):
    for kd in range(3):
        line = {}
        for pw in range(2):
            for b in range(2):
                row = pl.multiple_of(kd * 64 + b * 32 + base, 16)
                part = [
                    g_ref[k, pw, pl.ds(row, 16), c * 128 : c * 128 + 128]
                    for c in range(4)
                ]
                for kh in range(3):
                    line[pw, b, kh] = part[OFFSET[0][kh]] + part[2 + OFFSET[1][kh]]
        for kh in range(3):
            for kw in range(3):
                store(
                    9 * kd + 3 * kh + kw,
                    line[0, OFFSET[0][kw], kh] + line[1, OFFSET[1][kw], kh],
                )


def whole_kernel(
    scale, counts_any, w_any, x_any, cot_any, bias_any, o_any, b_ref,
    counts_ref, w_raw, w_pair, x_raw, cot_raw, bias_ref,
    wf_ref, f_ref, cf_ref, cp_ref, xs_ref, xt_ref, wz_ref, y_ref, dz_ref, g_ref,
    w_all, parts, s1, r1, s2, r2, keep, s3, r3, last, sb, rb,
    fetch, sw3, rw3, sw1, rw1, sw2, rw2, ss1, rs1, ss2, rs2, ss3, rs3, ss4, rs4, ssb, rsb,
):
    grp = lax.axis_index("grp")
    dev = lax.axis_index("dev")
    depth = dev // 2
    core = dev % 2
    f32, bf16 = jnp.float32, jnp.bfloat16
    masks = (3, 2, 1)
    pair = {"dev": depth * 2 + (1 - core)}
    across = [{"grp": xor(grp, m)} for m in masks]
    along = [{"dev": xor(depth, m) * 2 + core} for m in masks]

    barrier = pltpu.get_barrier_semaphore()
    for peer in along + across + [pair]:
        pl.semaphore_signal(barrier, inc=1, device_id=peer, device_id_type=MESH)

    fetches = []
    for i, (src, dst) in enumerate(
        (
            (w_any, w_raw),
            (cot_any, cot_raw),
            (x_any, x_raw),
            (bias_any, bias_ref),
            (counts_any, counts_ref),
        )
    ):
        fetches.append(pltpu.make_async_copy(src, dst, fetch.at[i]))
        fetches[i].start()

    def send(src, dst, ssem, rsem, peer):
        copy = pltpu.make_async_remote_copy(
            src_ref=src, dst_ref=dst, send_sem=ssem, recv_sem=rsem,
            device_id=peer, device_id_type=MESH,
        )
        copy.start()
        return copy

    pl.semaphore_wait(barrier, 7)

    fetches[0].wait()
    quarter = w_raw.at[pl.ds(pl.multiple_of((7 * grp - grp // 3) * 16, 16), 112)]
    out = [
        send(quarter, w_all.at[dev, grp], sw1.at[k], rw1.at[k], along[k])
        for k in range(3)
    ]
    swap = [send(w_raw, w_pair, sw2.at[3], rw2.at[3], pair)]
    clear_edges(dz_ref)
    zero = jnp.zeros((16, 128), bf16)
    for k in range(4):
        s1[k, 27] = zero
        parts[k, 27] = jnp.zeros((16, 128), f32)
    wf_ref[0] = w_raw[...].astype(f32)
    combine_shard(wf_ref.at[0], dev, wz_ref)
    fetches[1].wait()
    lay_out_cotangent(cot_raw, cf_ref, cp_ref)
    spread = {}
    for k in (2, 1, 0):
        out[k].wait_recv()
        block = w_all.at[xor(depth, masks[k]) * 2 + core, grp]
        for j in range(3):
            spread[k, j] = send(block, block, sw3.at[k, j], rw3.at[k, j], across[j])
    fetches[2].wait()
    lay_out_tiles(x_raw, f_ref, xs_ref, xt_ref)
    swap[0].wait_recv()
    wf_ref[1] = w_pair[...].astype(f32)
    combine_shard(wf_ref.at[1], depth * 2 + 1 - core, wz_ref)
    for k in (2, 1, 0):
        for j in range(3):
            spread[k, j].wait_recv()
        block = w_all.at[xor(depth, masks[k]) * 2 + core]
        swap.append(send(block, block, sw2.at[k], rw2.at[k], pair))
        spread_rows(w_all, xor(depth, masks[k]) * 2 + core, wf_ref.at[0])
        combine_shard(wf_ref.at[0], xor(depth, masks[k]) * 2 + core, wz_ref)
    for i, k in enumerate((2, 1, 0)):
        swap[1 + i].wait_recv()
        spread_rows(w_all, xor(depth, masks[k]) * 2 + 1 - core, wf_ref.at[1])
        combine_shard(wf_ref.at[1], xor(depth, masks[k]) * 2 + 1 - core, wz_ref)
    fetches[3].wait()
    fetches[4].wait()
    total_b = forward(
        counts_ref[grp * 8 + dev], xs_ref, wz_ref, y_ref, cp_ref, bias_ref, dz_ref
    )

    sb[0] = jnp.broadcast_to(total_b, (8, 128))
    bias_start = send(sb.at[0], rb.at[0], ssb.at[0], rsb.at[0], pair)
    for copy in out + list(spread.values()) + swap:
        copy.wait_send()

    def reduce_all(early):
        first, second, third = {}, {}, {}
        after = [1 - (depth - k + 2) // 3 for k in range(3)]
        goal = [k + after[k] for k in range(3)] + [depth]
        place = [depth - 1 + after[k] for k in range(3)]

        def work(k):
            backward(xt_ref, goal[k], dz_ref, g_ref, k)

        def give(k):
            def to_pair(tap, value):
                s1[k, tap] = value.astype(bf16)

            tap_sums(g_ref, k, 16 if early else 0, to_pair)
            first[k] = send(s1.at[k], r1.at[k], ss1.at[k], rs1.at[k], pair)

        def own(k):
            def to_self(tap, value):
                parts[k, tap] = value

            tap_sums(g_ref, k, 0 if early else 16, to_self)

        def start_second(k):
            arrived = pltpu.make_async_remote_copy(
                src_ref=s1.at[k], dst_ref=r1.at[k], send_sem=ss1.at[k], recv_sem=rs1.at[k],
                device_id=pair, device_id_type=MESH,
            )
            arrived.wait_recv()
            for j in range(4):
                owner = xor(grp, masks[j]) if j < 3 else grp
                taps = pl.ds(owner * 7, 7)
                total = parts[k, taps] + r1[k, taps].astype(f32)
                if j < 3:
                    s2[k, j] = total.astype(bf16)
                    second[k, j] = send(
                        s2.at[k, j], r2.at[k, j], ss2.at[k, j], rs2.at[k, j], across[j]
                    )
                else:
                    keep[k] = total

        def start_third(k):
            total = keep[k]
            for j in range(3):
                second[k, j].wait_recv()
                total += r2[k, j].astype(f32)
            if k < 3:
                s3[k] = total.astype(bf16)
                third[k] = send(
                    s3.at[k], r3.at[place[k]], ss3.at[k], rs3.at[place[k]],
                    {"dev": goal[k] * 2 + core},
                )
            else:
                keep[k] = total

        bias_copies = []

        def bias_across():
            bias_start.wait_recv()
            sb[1] = sb[0] + rb[0]
            for k in range(3):
                bias_copies.append(
                    send(sb.at[1], rb.at[1 + k], ssb.at[1 + k], rsb.at[1 + k], across[k])
                )

        def bias_along():
            for k in range(3):
                bias_copies[k].wait_recv()
            sb[2] = (sb[1] + rb[3]) + (rb[2] + rb[1])
            for k in range(3):
                bias_copies.append(
                    send(sb.at[2], rb.at[4 + k], ssb.at[4 + k], rsb.at[4 + k], along[k])
                )

        if early:
            work(0)
            own(0)
            work(1)
            own(1)
            start_second(0)
            work(2)
            own(2)
            start_second(1)
            give(0)
            work(3)
            own(3)
            start_second(2)
            start_second(3)
            give(1)
            give(2)
            give(3)
            bias_across()
        else:
            for k in range(4):
                work(k)
                give(k)
            bias_across()
            for k in range(4):
                own(k)
                start_second(k)
        start_third(0)
        start_third(1)
        start_third(2)
        bias_along()
        start_third(3)
        total = keep[3]
        for k in range(3):
            pltpu.make_async_remote_copy(
                src_ref=s3.at[k], dst_ref=r3.at[k], send_sem=ss3.at[k], recv_sem=rs3.at[k],
                device_id=along[k], device_id_type=MESH,
            ).wait_recv()
            total += r3[k].astype(f32)
        last[...] = (total * scale).astype(bf16)
        fourth = [
            send(last, o_any.at[grp], ss4.at[k], rs4.at[k], across[k]) for k in range(3)
        ]
        mine = pltpu.make_async_copy(last, o_any.at[grp], fetch.at[5])
        mine.start()
        for k in range(3):
            bias_copies[3 + k].wait_recv()
        whole_b = (((sb[2] + rb[6]) + (rb[5] + rb[4])) * scale)[0:1]
        share = jnp.zeros((1, 16), f32)
        for d in range(8):
            share = jnp.where(dev == d, whole_b[:, d * 16 : d * 16 + 16], share)
        b_ref[...] = share
        for copy in list(first.values()) + list(second.values()) + list(third.values()):
            copy.wait_send()
        for copy in [bias_start] + bias_copies + fourth:
            copy.wait_send()
        mine.wait()
        for k in (2, 1, 0):
            fourth[k].wait_recv()

    @pl.when(core == 0)
    def _():
        reduce_all(True)

    @pl.when(core == 1)
    def _():
        reduce_all(False)


def whole(counts, w, x, cot, bias, scale):
    bf16, f32 = jnp.bfloat16, jnp.float32
    sem = pltpu.SemaphoreType.DMA
    vmem = pltpu.VMEM
    return pl.pallas_call(
        functools.partial(whole_kernel, scale),
        out_shape=(
            jax.ShapeDtypeStruct((4, 7, 16, 128), bf16),
            jax.ShapeDtypeStruct((1, 16), f32),
        ),
        in_specs=[pl.BlockSpec(memory_space=pltpu.HBM)] * 5,
        out_specs=[
            pl.BlockSpec(memory_space=pltpu.HBM),
            pl.BlockSpec(memory_space=pltpu.VMEM),
        ],
        scratch_shapes=[
            pltpu.SMEM((32,), jnp.int32),
            vmem((432, 128), bf16),
            vmem((432, 128), bf16),
            vmem((576, 128), bf16),
            vmem((2304, 128), bf16),
            vmem((1, 128), f32),
            vmem((2, 432, 128), f32),
            vmem((3, 592, 128), f32),
            vmem((8, 288, 128), f32),
            vmem((4, 576, 128), f32),
            vmem((2, 576, 768), bf16),
            vmem((4, 2, 192, 576), bf16),
            vmem((2, 768, 512), bf16),
            vmem((4, 576, 256), f32),
            vmem((2, 576, 512), bf16),
            vmem((4, 2, 192, 512), f32),
            vmem((8, 4, 112, 128), bf16),
            vmem((4, 28, 16, 128), f32),
            vmem((4, 28, 16, 128), bf16),
            vmem((4, 28, 16, 128), bf16),
            vmem((4, 3, 7, 16, 128), bf16),
            vmem((4, 3, 7, 16, 128), bf16),
            vmem((4, 7, 16, 128), f32),
            vmem((3, 7, 16, 128), bf16),
            vmem((3, 7, 16, 128), bf16),
            vmem((7, 16, 128), bf16),
            vmem((3, 8, 128), f32),
            vmem((7, 8, 128), f32),
            sem((6,)), sem((3, 3)), sem((3, 3)),
            sem((3,)), sem((3,)), sem((4,)), sem((4,)),
            sem((4,)), sem((4,)), sem((4, 3)), sem((4, 3)),
            sem((3,)), sem((3,)), sem((3,)), sem((3,)),
            sem((7,)), sem((7,)),
        ],
        compiler_params=pltpu.CompilerParams(
            collective_id=1, has_side_effects=True, vmem_limit_bytes=60 * 2**20
        ),
    )(counts, w, x, cot, bias)


def sort_rows_kernel(w_ref, b_ref, o_any, p_any, rows_ref, sems):
    bias = pltpu.make_async_copy(b_ref, p_any, sems.at[1])
    bias.start()
    for k in range(27):
        rows_ref[pl.ds(k, 16, 27), :] = w_ref[k // 7, k % 7].astype(jnp.float32)
    copy = pltpu.make_async_copy(rows_ref, o_any, sems.at[0])
    copy.start()
    bias.wait()
    copy.wait()


def sort_rows(part_w, part_b):
    f32 = jnp.float32
    return pl.pallas_call(
        sort_rows_kernel,
        out_shape=(
            jax.ShapeDtypeStruct((432, 128), f32),
            jax.ShapeDtypeStruct(part_b.shape, f32),
        ),
        in_specs=[pl.BlockSpec(memory_space=pltpu.VMEM)] * 2,
        out_specs=[pl.BlockSpec(memory_space=pltpu.HBM)] * 2,
        scratch_shapes=[pltpu.VMEM((432, 128), f32), pltpu.SemaphoreType.DMA((2,))],
    )(part_w, part_b)


def body(tiles, cotangent, weight, bias, counts):
    num_dev = lax.axis_size("dev")
    num_grp = lax.axis_size("grp")
    cap, frames, hl, wl, cin = tiles.shape
    cout = weight.shape[1]
    my_dev = lax.axis_index("dev")
    my_grp = lax.axis_index("grp")
    scale = 1.0 / math.sqrt(cap * num_dev * num_grp * frames * 4 * hl * wl)
    bias = bias.reshape(1, cout)
    if (num_grp, num_dev) == (4, 8):
        x = tiles.reshape(cap * frames * hl * wl, cin)
        cot = cotangent.reshape(cap * frames * 4 * hl * wl, cout)
        part_w, part_b = sort_rows(*whole(counts, weight, x, cot, bias, scale))
        return part_w, part_b.reshape(cout // num_dev)

    mine = weight.reshape(cin // num_dev, 27, cout).transpose(1, 0, 2)
    x = tiles.transpose(2, 3, 0, 1, 4).reshape(hl * wl * cap * frames, cin)
    cot = cotangent.reshape(cap, frames, hl, 2, wl, 2, cout).transpose(3, 5, 2, 4, 0, 1, 6)
    cot = cot.reshape(4, hl * wl * cap * frames, cout)
    share = cout // num_dev
    gathered = lax.all_gather(mine, "dev", axis=0, tiled=False)
    if num_dev != 8:
        gathered = gathered.transpose(1, 0, 2, 3).reshape(27, 8, 16, cout)
        gathered = gathered.transpose(1, 0, 2, 3)
    count = lax.dynamic_slice_in_dim(counts, my_grp * num_dev + my_dev, 1)
    parts = terms(count, gathered, x, cot, bias)
    flat = parts[:, :27].transpose(0, 2, 1, 3).reshape(cin * 27, cout)
    part_w = lax.psum_scatter(flat, "dev", scatter_dimension=0, tiled=True)
    part_w = lax.psum(part_w, "grp")
    total_b = lax.psum(parts[0, 27, 0], ("grp", "dev"))
    part_b = lax.dynamic_slice_in_dim(total_b, my_dev * share, share, 0)
    return part_w * scale, part_b * scale


def solution(mesh):
    return jax.shard_map(
        body,
        mesh=mesh,
        in_specs=(
            P(("grp", "dev"), None, None, None, None),
            P(("grp", "dev"), None, None, None, None),
            P("dev", None),
            P(),
            P(),
        ),
        out_specs=(P("dev", None), P("dev")),
        check_vma=False,
    )
```

```python
import functools
import math

import jax
import jax.numpy as jnp
from jax import lax
from jax.experimental import pallas as pl
from jax.experimental.pallas import tpu as pltpu
from jax.sharding import PartitionSpec as P

MESH = pl.DeviceIdType.MESH
TAPS = {(0, 0): (0,), (0, 1): (1, 2), (1, 0): (0, 1), (1, 1): (2,)}
OFFSET = ((0, 1, 1), (0, 0, 1))


def build_windows(x_ref, f_ref, xs_ref):
    rows = x_ref.shape[0]
    slab = rows // 4
    pad = 40
    row = lax.broadcasted_iota(jnp.int32, (rows, 128), 0).astype(jnp.float32)
    frame = row - 9.0 * jnp.floor((row + 0.5) * (1.0 / 9.0))
    place = lax.broadcasted_iota(jnp.int32, (slab, 128), 0)
    xs_ref[0:slab] = jnp.zeros((slab, 1152), jnp.bfloat16)
    xs_ref[5 * slab : 6 * slab] = jnp.zeros((slab, 1152), jnp.bfloat16)
    f_ref[...] = jnp.zeros_like(f_ref)
    now = x_ref[...].astype(jnp.float32)
    f_ref[2, pad : pad + rows] = now
    back1 = jnp.where(frame < 0.5, now, f_ref[2, pad - 1 : pad - 1 + rows])
    f_ref[1, pad : pad + rows] = back1
    f_ref[0, pad : pad + rows] = jnp.where(
        frame < 1.5, back1, f_ref[2, pad - 2 : pad - 2 + rows]
    )
    for h in range(4):
        for dw in range(3):
            for kd in range(3):
                start = pad + h * slab + (dw - 1) * 36
                piece = f_ref[kd, start : start + slab]
                if dw == 0:
                    piece = jnp.where(place < 36, 0.0, piece)
                if dw == 2:
                    piece = jnp.where(place >= slab - 36, 0.0, piece)
                col = dw * 384 + kd * 128
                xs_ref[(h + 1) * slab : (h + 2) * slab, col : col + 128] = piece.astype(
                    jnp.bfloat16
                )


def combine_weights(w_ref, wz_ref):
    chans = 128
    for kd in range(3):
        tap = {}
        for kh in range(3):
            for kw in range(3):
                piece = w_ref[:, 9 * kd + 3 * kh + kw]
                tap[kh, kw] = piece.reshape(chans, chans).astype(jnp.float32)
        for ph in range(2):
            for a in range(2):
                line = [sum(tap[kh, kw] for kh in TAPS[ph, a]) for kw in range(3)]
                for pw in range(2):
                    for b in range(2):
                        both = sum(line[kw] for kw in TAPS[pw, b])
                        row = (b + pw) * 384 + kd * 128
                        col = (2 * ph + pw) * 128
                        wz_ref[a + ph, row : row + 128, col : col + 128] = both.astype(
                            jnp.bfloat16
                        )


def products(count, xs_ref, cot_ref, bias_ref, wz_ref, g_ref):
    slab = xs_ref.shape[0] // 6
    rows = 4 * slab
    row = lax.broadcasted_iota(jnp.int32, (rows, 128), 0).astype(jnp.float32)
    place = row - 36.0 * jnp.floor((row + 0.5) * (1.0 / 36.0))
    live = place < 9.0 * count.astype(jnp.float32)
    cols = ((0, 256), (0, 512), (256, 256))

    def window(dh):
        return xs_ref[dh * slab : dh * slab + rows, :]

    mid = jnp.dot(window(1), wz_ref[1], preferred_element_type=jnp.float32)
    top = jnp.dot(window(0), wz_ref[0, :, 0:256], preferred_element_type=jnp.float32)
    low = jnp.dot(window(2), wz_ref[2, :, 256:512], preferred_element_type=jnp.float32)
    parts = []
    total_b = jnp.zeros((1, 128), jnp.float32)
    for p in range(4):
        side = (top if p < 2 else low)[:, (p % 2) * 128 : (p % 2) * 128 + 128]
        z = mid[:, p * 128 : p * 128 + 128] + side + bias_ref[...]
        sig = jax.nn.sigmoid(z)
        dz = cot_ref[p].astype(jnp.float32) * sig * (1.0 + z * (1.0 - sig))
        dz = jnp.where(live, dz, 0.0).astype(jnp.bfloat16)
        total_b += jnp.sum(dz.astype(jnp.float32), axis=0, keepdims=True)
        parts.append(dz)
    dz = jnp.concatenate(parts, axis=1)
    for dh in range(3):
        start, width = cols[dh]
        g_ref[dh, :, start : start + width] = lax.dot_general(
            window(dh),
            dz[:, start : start + width],
            (((0,), (0,)), ((), ())),
            preferred_element_type=jnp.float32,
        )
    return total_b


def tap_gradient(g_ref, k, base=0, size=128):
    kd, kh, kw = k // 9, k // 3 % 3, k % 3
    total = None
    for ph in range(2):
        for pw in range(2):
            row = (OFFSET[pw][kw] + pw) * 384 + kd * 128
            col = (2 * ph + pw) * 128
            term = g_ref[
                OFFSET[ph][kh] + ph, pl.ds(base + row, size), col : col + 128
            ]
            total = term if total is None else total + term
    return total


WORK = [
    pltpu.VMEM((3, 656, 128), jnp.float32),
    pltpu.VMEM((864, 1152), jnp.bfloat16),
    pltpu.VMEM((3, 1152, 512), jnp.bfloat16),
    pltpu.VMEM((3, 1152, 512), jnp.float32),
]


def terms_kernel(
    count_ref, w_ref, x_ref, cot_ref, bias_ref, out_ref, f_ref, xs_ref, wz_ref, g_ref
):
    build_windows(x_ref, f_ref, xs_ref)
    wz_ref[...] = jnp.zeros_like(wz_ref)
    combine_weights(w_ref, wz_ref)
    total_b = products(count_ref[0], xs_ref, cot_ref, bias_ref, wz_ref, g_ref)
    for k in range(27):
        out_ref[:, k] = tap_gradient(g_ref, k).reshape(8, 16, 128)
    out_ref[:, 27] = jnp.broadcast_to(total_b.reshape(1, 1, 128), (8, 16, 128))


def terms(count, w, x, cot, bias):
    return pl.pallas_call(
        terms_kernel,
        out_shape=jax.ShapeDtypeStruct((8, 28, 16, 128), jnp.float32),
        in_specs=[pl.BlockSpec(memory_space=pltpu.SMEM)]
        + [pl.BlockSpec(memory_space=pltpu.VMEM)] * 4,
        out_specs=pl.BlockSpec(memory_space=pltpu.VMEM),
        scratch_shapes=WORK,
        compiler_params=pltpu.CompilerParams(vmem_limit_bytes=48 * 2**20),
    )(count, w, x, cot, bias)


def xor(value, mask):
    if mask == 1:
        return value + 1 - 2 * (value % 2)
    if mask == 2:
        return (value + 2) % 4
    return 3 - value


def lay_out_tiles(x_raw, f_ref, xs_ref, xt_ref):
    pad = 8
    rows = 576
    full = x_raw[...].astype(jnp.float32)
    for tf in range(36):
        for h in range(4):
            at = pad + h * 144 + tf * 4
            f_ref[2, at : at + 4] = full[tf * 16 + h * 4 : tf * 16 + h * 4 + 4]
    row = lax.broadcasted_iota(jnp.int32, (144, 128), 0)
    w = row % 4
    frame = (row // 4) % 9
    for h in range(4):
        at = pad + h * 144
        now = f_ref[2, at : at + 144]
        back1 = jnp.where(frame < 1, now, f_ref[2, at - 4 : at + 140])
        back2 = jnp.where(frame < 2, back1, f_ref[2, at - 8 : at + 136])
        f_ref[1, at : at + 144] = back1
        f_ref[0, at : at + 144] = back2
    for kd in range(3):
        for h in range(4):
            at = pad + h * 144
            lines = slice(h * 144, h * 144 + 144)
            left = jnp.where(w == 0, 0.0, f_ref[kd, at - 1 : at + 143])
            here = f_ref[kd, at : at + 144]
            right = jnp.where(w == 3, 0.0, f_ref[kd, at + 1 : at + 145])
            left, here, right = (
                piece.astype(jnp.bfloat16) for piece in (left, here, right)
            )
            col = kd * 256
            xs_ref[0, lines, col : col + 128] = left
            xs_ref[0, lines, col + 128 : col + 256] = here
            xs_ref[1, lines, col : col + 128] = here
            xs_ref[1, lines, col + 128 : col + 256] = right
    for kd in range(3):
        for pw in range(2):
            for b in range(2):
                col = kd * 256 + b * 128
                if (pw, b) == (1, 0):
                    continue
                block = xs_ref[pw, :, col : col + 128].astype(jnp.float32).T
                block = block.astype(jnp.bfloat16)
                for part in range(4):
                    piece = block[part * 32 : part * 32 + 32]
                    at = kd * 64 + b * 32
                    xt_ref[part, pw, at : at + 32, :] = piece
                    if (pw, b) == (0, 1):
                        xt_ref[part, 1, kd * 64 : kd * 64 + 32, :] = piece


def lay_out_cotangent(count, cot_raw, cf_ref, cp_ref):
    live = lax.broadcasted_iota(jnp.int32, (144, 128), 0) < 36 * count
    for tf in range(36):
        full = cot_raw[tf * 64 : tf * 64 + 64].astype(jnp.float32)
        for line in range(8):
            cf_ref[line, tf * 8 : tf * 8 + 8] = full[line * 8 : line * 8 + 8]
    for h in range(4):
        for ph in range(2):
            for pw in range(2):
                here = cf_ref[2 * h + ph, pl.ds(pw, 144, 2), :]
                cp_ref[2 * ph + pw, h * 144 : h * 144 + 144] = jnp.where(
                    live, 0.5 * here, 0.0
                )


def spread_rows(w_ref, d, wf_ref):
    for q in range(4):
        at = (7 * q - q // 3) * 16
        wf_ref[at : at + 112] = w_ref[d, q].astype(jnp.float32)


def combine_shard(wf_ref, d, wz_ref):
    for kd in range(3):
        tap = {}
        for kh in range(3):
            for kw in range(3):
                tap[kh, kw] = 0.5 * wf_ref[pl.ds(9 * kd + 3 * kh + kw, 16, 27), :]
        for ph in range(2):
            for a in range(2):
                line = [sum(tap[kh, kw] for kh in TAPS[ph, a]) for kw in range(3)]
                for pw in range(2):
                    for b in range(2):
                        both = sum(line[kw] for kw in TAPS[pw, b])
                        row = pl.multiple_of(kd * 256 + b * 128 + d * 16, 16)
                        col = (2 * ph + a) * 128
                        wz_ref[pw, pl.ds(row, 16), col : col + 128] = both.astype(
                            jnp.bfloat16
                        )


def forward(xs_ref, wz_ref, y_ref, cp_ref, bias_ref, dz_ref):
    f32 = jnp.float32
    units = [(pw, ph) for pw in range(2) for ph in range(2)]
    totals = []

    def multiply(pw, ph):
        y_ref[2 * pw + ph] = jnp.dot(
            xs_ref[pw],
            wz_ref[pw, :, ph * 256 : ph * 256 + 256],
            preferred_element_type=f32,
        )

    def finish(pw, ph):
        for h in range(4):
            half = 0.5 * bias_ref[...]
            for a in range(2):
                s = h + a + ph - 1
                if 0 <= s < 4:
                    half = half + y_ref[
                        2 * pw + ph, s * 144 : s * 144 + 144, a * 128 : a * 128 + 128
                    ]
            t = jnp.tanh(half)
            lines = slice(h * 144, h * 144 + 144)
            dz = cp_ref[2 * ph + pw, lines] * (1.0 + t) * (1.0 + half * (1.0 - t))
            dz = dz.astype(jnp.bfloat16)
            totals.append(jnp.sum(dz.astype(f32), axis=0, keepdims=True))
            for a in range(2):
                s = h + a + ph - 1
                if 0 <= s < 4:
                    col = ph * 256 + a * 128
                    dz_ref[pw, s * 144 : s * 144 + 144, col : col + 128] = dz

    multiply(*units[0])
    for step in range(4):
        if step < 3:
            multiply(*units[step + 1])
        finish(*units[step])
    return sum(totals)


def clear_edges(dz_ref):
    zero = jnp.zeros((144, 128), jnp.bfloat16)
    for pw in range(2):
        dz_ref[pw, 432:576, 0:128] = zero
        dz_ref[pw, 0:144, 384:512] = zero


def backward(xt_ref, part, dz_ref, g_ref, k):
    for pw in range(2):
        g_ref[k, pw] = jnp.dot(
            xt_ref[part, pw], dz_ref[pw], preferred_element_type=jnp.float32
        )


def tap_sums(g_ref, k, base, store):
    for kd in range(3):
        line = {}
        for pw in range(2):
            for b in range(2):
                row = pl.multiple_of(kd * 64 + b * 32 + base, 16)
                part = [
                    g_ref[k, pw, pl.ds(row, 16), c * 128 : c * 128 + 128]
                    for c in range(4)
                ]
                for kh in range(3):
                    line[pw, b, kh] = part[OFFSET[0][kh]] + part[2 + OFFSET[1][kh]]
        for kh in range(3):
            for kw in range(3):
                store(
                    9 * kd + 3 * kh + kw,
                    line[0, OFFSET[0][kw], kh] + line[1, OFFSET[1][kw], kh],
                )


def whole_kernel(
    scale, counts_any, w_any, x_any, cot_any, bias_any, o_any, b_ref,
    counts_ref, w_raw, w_pair, x_raw, cot_raw, bias_ref,
    wf_ref, f_ref, cf_ref, cp_ref, xs_ref, xt_ref, wz_ref, y_ref, dz_ref, g_ref,
    w_all, parts, s1, r1, s2, r2, keep, s3, r3, last, sb, rb,
    fetch, sw3, rw3, sw1, rw1, sw2, rw2, ss1, rs1, ss2, rs2, ss3, rs3, ss4, rs4, ssb, rsb, ready,
):
    grp = lax.axis_index("grp")
    dev = lax.axis_index("dev")
    depth = dev // 2
    core = dev % 2
    f32, bf16 = jnp.float32, jnp.bfloat16
    masks = (3, 2, 1)
    pair = {"dev": depth * 2 + (1 - core)}
    across = [{"grp": xor(grp, m)} for m in masks]
    along = [{"dev": xor(depth, m) * 2 + core} for m in masks]

    barrier = pltpu.get_barrier_semaphore()
    for peer in along + across:
        pl.semaphore_signal(barrier, inc=1, device_id=peer, device_id_type=MESH)

    @pl.when(core == 0)
    def _():
        pl.semaphore_signal(barrier, inc=1, device_id=pair, device_id_type=MESH)

    fetches = []
    for i, (src, dst) in enumerate(
        (
            (w_any, w_raw),
            (cot_any, cot_raw),
            (x_any, x_raw),
            (bias_any, bias_ref),
            (counts_any, counts_ref),
        )
    ):
        fetches.append(pltpu.make_async_copy(src, dst, fetch.at[i]))
        fetches[i].start()

    def send(src, dst, ssem, rsem, peer):
        copy = pltpu.make_async_remote_copy(
            src_ref=src, dst_ref=dst, send_sem=ssem, recv_sem=rsem,
            device_id=peer, device_id_type=MESH,
        )
        copy.start()
        return copy

    pl.semaphore_wait(barrier, 6 + core)

    @pl.when(core == 1)
    def _():
        pl.semaphore_signal(ready, inc=1, device_id=pair, device_id_type=MESH)

    fetches[0].wait()
    quarter = w_raw.at[pl.ds(pl.multiple_of((7 * grp - grp // 3) * 16, 16), 112)]
    out = [
        send(quarter, w_all.at[dev, grp], sw1.at[k], rw1.at[k], along[k])
        for k in range(3)
    ]
    clear_edges(dz_ref)
    zero = jnp.zeros((16, 128), bf16)
    for k in range(4):
        s1[k, 27] = zero
        parts[k, 27] = jnp.zeros((16, 128), f32)
    wf_ref[0] = w_raw[...].astype(f32)
    combine_shard(wf_ref.at[0], dev, wz_ref)
    fetches[1].wait()
    fetches[4].wait()
    lay_out_cotangent(counts_ref[grp * 8 + dev], cot_raw, cf_ref, cp_ref)
    spread = {}
    for k in (2, 1, 0):
        out[k].wait_recv()
        block = w_all.at[xor(depth, masks[k]) * 2 + core, grp]
        for j in range(3):
            spread[k, j] = send(block, block, sw3.at[k, j], rw3.at[k, j], across[j])

    @pl.when(core == 0)
    def _():
        pl.semaphore_wait(ready, 1)

    swap = [send(w_raw, w_pair, sw2.at[3], rw2.at[3], pair)]
    fetches[2].wait()
    lay_out_tiles(x_raw, f_ref, xs_ref, xt_ref)
    swap[0].wait_recv()
    wf_ref[1] = w_pair[...].astype(f32)
    combine_shard(wf_ref.at[1], depth * 2 + 1 - core, wz_ref)
    for k in (2, 1, 0):
        for j in range(3):
            spread[k, j].wait_recv()
        block = w_all.at[xor(depth, masks[k]) * 2 + core]
        swap.append(send(block, block, sw2.at[k], rw2.at[k], pair))
        spread_rows(w_all, xor(depth, masks[k]) * 2 + core, wf_ref.at[0])
        combine_shard(wf_ref.at[0], xor(depth, masks[k]) * 2 + core, wz_ref)
    for i, k in enumerate((2, 1, 0)):
        swap[1 + i].wait_recv()
        spread_rows(w_all, xor(depth, masks[k]) * 2 + 1 - core, wf_ref.at[1])
        combine_shard(wf_ref.at[1], xor(depth, masks[k]) * 2 + 1 - core, wz_ref)
    fetches[3].wait()
    total_b = forward(xs_ref, wz_ref, y_ref, cp_ref, bias_ref, dz_ref)

    sb[0] = jnp.broadcast_to(total_b, (8, 128))
    bias_start = send(sb.at[0], rb.at[0], ssb.at[0], rsb.at[0], pair)
    for copy in out + list(spread.values()) + swap:
        copy.wait_send()

    def reduce_all(early):
        first, second, third = {}, {}, {}
        after = [1 - (depth - k + 2) // 3 for k in range(3)]
        goal = [k + after[k] for k in range(3)] + [depth]
        place = [depth - 1 + after[k] for k in range(3)]

        def work(k):
            backward(xt_ref, goal[k], dz_ref, g_ref, k)

        def give(k):
            def to_pair(tap, value):
                s1[k, tap] = value.astype(bf16)

            tap_sums(g_ref, k, 16 if early else 0, to_pair)
            first[k] = send(s1.at[k], r1.at[k], ss1.at[k], rs1.at[k], pair)

        def own(k):
            def to_self(tap, value):
                parts[k, tap] = value

            tap_sums(g_ref, k, 0 if early else 16, to_self)

        def start_second(k):
            arrived = pltpu.make_async_remote_copy(
                src_ref=s1.at[k], dst_ref=r1.at[k], send_sem=ss1.at[k], recv_sem=rs1.at[k],
                device_id=pair, device_id_type=MESH,
            )
            arrived.wait_recv()
            for j in range(4):
                owner = xor(grp, masks[j]) if j < 3 else grp
                taps = pl.ds(owner * 7, 7)
                total = parts[k, taps] + r1[k, taps].astype(f32)
                if j < 3:
                    s2[k, j] = total.astype(bf16)
                    second[k, j] = send(
                        s2.at[k, j], r2.at[k, j], ss2.at[k, j], rs2.at[k, j], across[j]
                    )
                else:
                    keep[k] = total

        def start_third(k):
            total = keep[k]
            for j in range(3):
                second[k, j].wait_recv()
                total += r2[k, j].astype(f32)
            if k < 3:
                s3[k] = total.astype(bf16)
                third[k] = send(
                    s3.at[k], r3.at[place[k]], ss3.at[k], rs3.at[place[k]],
                    {"dev": goal[k] * 2 + core},
                )
            else:
                keep[k] = total

        bias_copies = []

        def bias_across():
            bias_start.wait_recv()
            sb[1] = sb[0] + rb[0]
            for k in range(3):
                bias_copies.append(
                    send(sb.at[1], rb.at[1 + k], ssb.at[1 + k], rsb.at[1 + k], across[k])
                )

        def bias_along():
            for k in range(3):
                bias_copies[k].wait_recv()
            sb[2] = (sb[1] + rb[3]) + (rb[2] + rb[1])
            for k in range(3):
                bias_copies.append(
                    send(sb.at[2], rb.at[4 + k], ssb.at[4 + k], rsb.at[4 + k], along[k])
                )

        if early:
            work(0)
            own(0)
            work(1)
            own(1)
            start_second(0)
            work(2)
            own(2)
            start_second(1)
            give(0)
            work(3)
            own(3)
            start_second(2)
            start_second(3)
            give(1)
            give(2)
            give(3)
            bias_across()
        else:
            for k in range(4):
                work(k)
                give(k)
            bias_across()
            for k in range(4):
                own(k)
                start_second(k)
        start_third(0)
        start_third(1)
        start_third(2)
        bias_along()
        start_third(3)
        total = keep[3]
        for k in range(3):
            pltpu.make_async_remote_copy(
                src_ref=s3.at[k], dst_ref=r3.at[k], send_sem=ss3.at[k], recv_sem=rs3.at[k],
                device_id=along[k], device_id_type=MESH,
            ).wait_recv()
            total += r3[k].astype(f32)
        last[...] = (total * scale).astype(bf16)
        fourth = [
            send(last, o_any.at[grp], ss4.at[k], rs4.at[k], across[k]) for k in range(3)
        ]
        mine = pltpu.make_async_copy(last, o_any.at[grp], fetch.at[5])
        mine.start()
        for k in range(3):
            bias_copies[3 + k].wait_recv()
        whole_b = (((sb[2] + rb[6]) + (rb[5] + rb[4])) * scale)[0:1]
        share = jnp.zeros((1, 16), f32)
        for d in range(8):
            share = jnp.where(dev == d, whole_b[:, d * 16 : d * 16 + 16], share)
        b_ref[...] = share
        for copy in list(first.values()) + list(second.values()) + list(third.values()):
            copy.wait_send()
        for copy in [bias_start] + bias_copies + fourth:
            copy.wait_send()
        mine.wait()
        for k in (2, 1, 0):
            fourth[k].wait_recv()

    @pl.when(core == 0)
    def _():
        reduce_all(True)

    @pl.when(core == 1)
    def _():
        reduce_all(False)


def whole(counts, w, x, cot, bias, scale):
    bf16, f32 = jnp.bfloat16, jnp.float32
    sem = pltpu.SemaphoreType.DMA
    vmem = pltpu.VMEM
    return pl.pallas_call(
        functools.partial(whole_kernel, scale),
        out_shape=(
            jax.ShapeDtypeStruct((4, 7, 16, 128), bf16),
            jax.ShapeDtypeStruct((1, 16), f32),
        ),
        in_specs=[pl.BlockSpec(memory_space=pltpu.HBM)] * 5,
        out_specs=[
            pl.BlockSpec(memory_space=pltpu.VMEM),
            pl.BlockSpec(memory_space=pltpu.VMEM),
        ],
        scratch_shapes=[
            pltpu.SMEM((32,), jnp.int32),
            vmem((432, 128), bf16),
            vmem((432, 128), bf16),
            vmem((576, 128), bf16),
            vmem((2304, 128), bf16),
            vmem((1, 128), f32),
            vmem((2, 432, 128), f32),
            vmem((3, 592, 128), f32),
            vmem((8, 288, 128), f32),
            vmem((4, 576, 128), f32),
            vmem((2, 576, 768), bf16),
            vmem((4, 2, 192, 576), bf16),
            vmem((2, 768, 512), bf16),
            vmem((4, 576, 256), f32),
            vmem((2, 576, 512), bf16),
            vmem((4, 2, 192, 512), f32),
            vmem((8, 4, 112, 128), bf16),
            vmem((4, 28, 16, 128), f32),
            vmem((4, 28, 16, 128), bf16),
            vmem((4, 28, 16, 128), bf16),
            vmem((4, 3, 7, 16, 128), bf16),
            vmem((4, 3, 7, 16, 128), bf16),
            vmem((4, 7, 16, 128), f32),
            vmem((3, 7, 16, 128), bf16),
            vmem((3, 7, 16, 128), bf16),
            vmem((7, 16, 128), bf16),
            vmem((3, 8, 128), f32),
            vmem((7, 8, 128), f32),
            sem((6,)), sem((3, 3)), sem((3, 3)),
            sem((3,)), sem((3,)), sem((4,)), sem((4,)),
            sem((4,)), sem((4,)), sem((4, 3)), sem((4, 3)),
            sem((3,)), sem((3,)), sem((3,)), sem((3,)),
            sem((7,)), sem((7,)), pltpu.SemaphoreType.REGULAR,
        ],
        compiler_params=pltpu.CompilerParams(
            collective_id=1, has_side_effects=True, vmem_limit_bytes=48 * 2**20
        ),
    )(*(pltpu.with_memory_space_constraint(v, pltpu.HBM) for v in (counts, w, x, cot, bias)))


def sort_rows_kernel(w_ref, b_ref, o_any, p_any, rows_ref, sems):
    bias = pltpu.make_async_copy(b_ref, p_any, sems.at[1])
    bias.start()
    for k in range(27):
        rows_ref[pl.ds(k, 16, 27), :] = w_ref[k // 7, k % 7].astype(jnp.float32)
    copy = pltpu.make_async_copy(rows_ref, o_any, sems.at[0])
    copy.start()
    bias.wait()
    copy.wait()


def sort_rows(part_w, part_b):
    f32 = jnp.float32
    return pl.pallas_call(
        sort_rows_kernel,
        out_shape=(
            jax.ShapeDtypeStruct((432, 128), f32),
            jax.ShapeDtypeStruct(part_b.shape, f32),
        ),
        in_specs=[pl.BlockSpec(memory_space=pltpu.VMEM)] * 2,
        out_specs=[pl.BlockSpec(memory_space=pltpu.HBM)] * 2,
        scratch_shapes=[pltpu.VMEM((432, 128), f32), pltpu.SemaphoreType.DMA((2,))],
        compiler_params=pltpu.CompilerParams(vmem_limit_bytes=4 * 2**20),
    )(part_w, part_b)


def body(tiles, cotangent, weight, bias, counts):
    num_dev = lax.axis_size("dev")
    num_grp = lax.axis_size("grp")
    cap, frames, hl, wl, cin = tiles.shape
    cout = weight.shape[1]
    my_dev = lax.axis_index("dev")
    my_grp = lax.axis_index("grp")
    scale = 1.0 / math.sqrt(cap * num_dev * num_grp * frames * 4 * hl * wl)
    bias = bias.reshape(1, cout)
    if (num_grp, num_dev) == (4, 8):
        x = tiles.reshape(cap * frames * hl * wl, cin)
        cot = cotangent.reshape(cap * frames * 4 * hl * wl, cout)
        part_w, part_b = sort_rows(*whole(counts, weight, x, cot, bias, scale))
        return part_w, part_b.reshape(cout // num_dev)

    mine = weight.reshape(cin // num_dev, 27, cout).transpose(1, 0, 2)
    x = tiles.transpose(2, 3, 0, 1, 4).reshape(hl * wl * cap * frames, cin)
    cot = cotangent.reshape(cap, frames, hl, 2, wl, 2, cout).transpose(3, 5, 2, 4, 0, 1, 6)
    cot = cot.reshape(4, hl * wl * cap * frames, cout)
    share = cout // num_dev
    gathered = lax.all_gather(mine, "dev", axis=0, tiled=False)
    if num_dev != 8:
        gathered = gathered.transpose(1, 0, 2, 3).reshape(27, 8, 16, cout)
        gathered = gathered.transpose(1, 0, 2, 3)
    count = lax.dynamic_slice_in_dim(counts, my_grp * num_dev + my_dev, 1)
    parts = terms(count, gathered, x, cot, bias)
    flat = parts[:, :27].transpose(0, 2, 1, 3).reshape(cin * 27, cout)
    part_w = lax.psum_scatter(flat, "dev", scatter_dimension=0, tiled=True)
    part_w = lax.psum(part_w, "grp")
    total_b = lax.psum(parts[0, 27, 0], ("grp", "dev"))
    part_b = lax.dynamic_slice_in_dim(total_b, my_dev * share, share, 0)
    return part_w * scale, part_b * scale


def solution(mesh):
    return jax.shard_map(
        body,
        mesh=mesh,
        in_specs=(
            P(("grp", "dev"), None, None, None, None),
            P(("grp", "dev"), None, None, None, None),
            P("dev", None),
            P(),
            P(),
        ),
        out_specs=(P("dev", None), P("dev")),
        check_vma=False,
    )
```

```python
import functools
import math

import jax
import jax.numpy as jnp
from jax import lax
from jax.experimental import pallas as pl
from jax.experimental.pallas import tpu as pltpu
from jax.sharding import PartitionSpec as P

MESH = pl.DeviceIdType.MESH
TAPS = {(0, 0): (0,), (0, 1): (1, 2), (1, 0): (0, 1), (1, 1): (2,)}
OFFSET = ((0, 1, 1), (0, 0, 1))


def build_windows(x_ref, f_ref, xs_ref):
    rows = x_ref.shape[0]
    slab = rows // 4
    pad = 40
    row = lax.broadcasted_iota(jnp.int32, (rows, 128), 0).astype(jnp.float32)
    frame = row - 9.0 * jnp.floor((row + 0.5) * (1.0 / 9.0))
    place = lax.broadcasted_iota(jnp.int32, (slab, 128), 0)
    xs_ref[0:slab] = jnp.zeros((slab, 1152), jnp.bfloat16)
    xs_ref[5 * slab : 6 * slab] = jnp.zeros((slab, 1152), jnp.bfloat16)
    f_ref[...] = jnp.zeros_like(f_ref)
    now = x_ref[...].astype(jnp.float32)
    f_ref[2, pad : pad + rows] = now
    back1 = jnp.where(frame < 0.5, now, f_ref[2, pad - 1 : pad - 1 + rows])
    f_ref[1, pad : pad + rows] = back1
    f_ref[0, pad : pad + rows] = jnp.where(
        frame < 1.5, back1, f_ref[2, pad - 2 : pad - 2 + rows]
    )
    for h in range(4):
        for dw in range(3):
            for kd in range(3):
                start = pad + h * slab + (dw - 1) * 36
                piece = f_ref[kd, start : start + slab]
                if dw == 0:
                    piece = jnp.where(place < 36, 0.0, piece)
                if dw == 2:
                    piece = jnp.where(place >= slab - 36, 0.0, piece)
                col = dw * 384 + kd * 128
                xs_ref[(h + 1) * slab : (h + 2) * slab, col : col + 128] = piece.astype(
                    jnp.bfloat16
                )


def combine_weights(w_ref, wz_ref):
    chans = 128
    for kd in range(3):
        tap = {}
        for kh in range(3):
            for kw in range(3):
                piece = w_ref[:, 9 * kd + 3 * kh + kw]
                tap[kh, kw] = piece.reshape(chans, chans).astype(jnp.float32)
        for ph in range(2):
            for a in range(2):
                line = [sum(tap[kh, kw] for kh in TAPS[ph, a]) for kw in range(3)]
                for pw in range(2):
                    for b in range(2):
                        both = sum(line[kw] for kw in TAPS[pw, b])
                        row = (b + pw) * 384 + kd * 128
                        col = (2 * ph + pw) * 128
                        wz_ref[a + ph, row : row + 128, col : col + 128] = both.astype(
                            jnp.bfloat16
                        )


def products(count, xs_ref, cot_ref, bias_ref, wz_ref, g_ref):
    slab = xs_ref.shape[0] // 6
    rows = 4 * slab
    row = lax.broadcasted_iota(jnp.int32, (rows, 128), 0).astype(jnp.float32)
    place = row - 36.0 * jnp.floor((row + 0.5) * (1.0 / 36.0))
    live = place < 9.0 * count.astype(jnp.float32)
    cols = ((0, 256), (0, 512), (256, 256))

    def window(dh):
        return xs_ref[dh * slab : dh * slab + rows, :]

    mid = jnp.dot(window(1), wz_ref[1], preferred_element_type=jnp.float32)
    top = jnp.dot(window(0), wz_ref[0, :, 0:256], preferred_element_type=jnp.float32)
    low = jnp.dot(window(2), wz_ref[2, :, 256:512], preferred_element_type=jnp.float32)
    parts = []
    total_b = jnp.zeros((1, 128), jnp.float32)
    for p in range(4):
        side = (top if p < 2 else low)[:, (p % 2) * 128 : (p % 2) * 128 + 128]
        z = mid[:, p * 128 : p * 128 + 128] + side + bias_ref[...]
        sig = jax.nn.sigmoid(z)
        dz = cot_ref[p].astype(jnp.float32) * sig * (1.0 + z * (1.0 - sig))
        dz = jnp.where(live, dz, 0.0).astype(jnp.bfloat16)
        total_b += jnp.sum(dz.astype(jnp.float32), axis=0, keepdims=True)
        parts.append(dz)
    dz = jnp.concatenate(parts, axis=1)
    for dh in range(3):
        start, width = cols[dh]
        g_ref[dh, :, start : start + width] = lax.dot_general(
            window(dh),
            dz[:, start : start + width],
            (((0,), (0,)), ((), ())),
            preferred_element_type=jnp.float32,
        )
    return total_b


def tap_gradient(g_ref, k, base=0, size=128):
    kd, kh, kw = k // 9, k // 3 % 3, k % 3
    total = None
    for ph in range(2):
        for pw in range(2):
            row = (OFFSET[pw][kw] + pw) * 384 + kd * 128
            col = (2 * ph + pw) * 128
            term = g_ref[
                OFFSET[ph][kh] + ph, pl.ds(base + row, size), col : col + 128
            ]
            total = term if total is None else total + term
    return total


WORK = [
    pltpu.VMEM((3, 656, 128), jnp.float32),
    pltpu.VMEM((864, 1152), jnp.bfloat16),
    pltpu.VMEM((3, 1152, 512), jnp.bfloat16),
    pltpu.VMEM((3, 1152, 512), jnp.float32),
]


def terms_kernel(
    count_ref, w_ref, x_ref, cot_ref, bias_ref, out_ref, f_ref, xs_ref, wz_ref, g_ref
):
    build_windows(x_ref, f_ref, xs_ref)
    wz_ref[...] = jnp.zeros_like(wz_ref)
    combine_weights(w_ref, wz_ref)
    total_b = products(count_ref[0], xs_ref, cot_ref, bias_ref, wz_ref, g_ref)
    for k in range(27):
        out_ref[:, k] = tap_gradient(g_ref, k).reshape(8, 16, 128)
    out_ref[:, 27] = jnp.broadcast_to(total_b.reshape(1, 1, 128), (8, 16, 128))


def terms(count, w, x, cot, bias):
    return pl.pallas_call(
        terms_kernel,
        out_shape=jax.ShapeDtypeStruct((8, 28, 16, 128), jnp.float32),
        in_specs=[pl.BlockSpec(memory_space=pltpu.SMEM)]
        + [pl.BlockSpec(memory_space=pltpu.VMEM)] * 4,
        out_specs=pl.BlockSpec(memory_space=pltpu.VMEM),
        scratch_shapes=WORK,
        compiler_params=pltpu.CompilerParams(vmem_limit_bytes=48 * 2**20),
    )(count, w, x, cot, bias)


def xor(value, mask):
    if mask == 1:
        return value + 1 - 2 * (value % 2)
    if mask == 2:
        return (value + 2) % 4
    return 3 - value


def lay_out_tiles(x_raw, f_ref, xs_ref, xt_ref):
    pad = 8
    rows = 576
    full = x_raw[...].astype(jnp.float32)
    for tf in range(36):
        for h in range(4):
            at = pad + h * 144 + tf * 4
            f_ref[2, at : at + 4] = full[tf * 16 + h * 4 : tf * 16 + h * 4 + 4]
    row = lax.broadcasted_iota(jnp.int32, (144, 128), 0)
    w = row % 4
    frame = (row // 4) % 9
    for h in range(4):
        at = pad + h * 144
        now = f_ref[2, at : at + 144]
        back1 = jnp.where(frame < 1, now, f_ref[2, at - 4 : at + 140])
        back2 = jnp.where(frame < 2, back1, f_ref[2, at - 8 : at + 136])
        f_ref[1, at : at + 144] = back1
        f_ref[0, at : at + 144] = back2
    for kd in range(3):
        for h in range(4):
            at = pad + h * 144
            lines = slice(h * 144, h * 144 + 144)
            left = jnp.where(w == 0, 0.0, f_ref[kd, at - 1 : at + 143])
            here = f_ref[kd, at : at + 144]
            right = jnp.where(w == 3, 0.0, f_ref[kd, at + 1 : at + 145])
            left, here, right = (
                piece.astype(jnp.bfloat16) for piece in (left, here, right)
            )
            col = kd * 256
            xs_ref[0, lines, col : col + 128] = left
            xs_ref[0, lines, col + 128 : col + 256] = here
            xs_ref[1, lines, col : col + 128] = here
            xs_ref[1, lines, col + 128 : col + 256] = right
    for kd in range(3):
        for pw in range(2):
            for b in range(2):
                col = kd * 256 + b * 128
                if (pw, b) == (1, 0):
                    continue
                block = xs_ref[pw, :, col : col + 128].astype(jnp.float32).T
                block = block.astype(jnp.bfloat16)
                for part in range(4):
                    piece = block[part * 32 : part * 32 + 32]
                    at = kd * 64 + b * 32
                    xt_ref[part, pw, at : at + 32, :] = piece
                    if (pw, b) == (0, 1):
                        xt_ref[part, 1, kd * 64 : kd * 64 + 32, :] = piece


def lay_out_cotangent(count, cot_raw, cf_ref, cp_ref):
    live = lax.broadcasted_iota(jnp.int32, (144, 128), 0) < 36 * count
    for tf in range(36):
        full = cot_raw[tf * 64 : tf * 64 + 64].astype(jnp.float32)
        for line in range(8):
            cf_ref[line, tf * 8 : tf * 8 + 8] = full[line * 8 : line * 8 + 8]
    for h in range(4):
        for ph in range(2):
            for pw in range(2):
                here = cf_ref[2 * h + ph, pl.ds(pw, 144, 2), :]
                cp_ref[2 * ph + pw, h * 144 : h * 144 + 144] = jnp.where(
                    live, 0.5 * here, 0.0
                )


def spread_rows(w_ref, d, wf_ref):
    for q in range(4):
        at = (7 * q - q // 3) * 16
        wf_ref[at : at + 112] = w_ref[d, q].astype(jnp.float32)


def combine_shard(wf_ref, d, wz_ref):
    for kd in range(3):
        tap = {}
        for kh in range(3):
            for kw in range(3):
                tap[kh, kw] = 0.5 * wf_ref[pl.ds(9 * kd + 3 * kh + kw, 16, 27), :]
        for ph in range(2):
            for a in range(2):
                line = [sum(tap[kh, kw] for kh in TAPS[ph, a]) for kw in range(3)]
                for pw in range(2):
                    for b in range(2):
                        both = sum(line[kw] for kw in TAPS[pw, b])
                        row = pl.multiple_of(kd * 256 + b * 128 + d * 16, 16)
                        col = (2 * ph + a) * 128
                        wz_ref[pw, pl.ds(row, 16), col : col + 128] = both.astype(
                            jnp.bfloat16
                        )


def forward(xs_ref, wz_ref, y_ref, cp_ref, bias_ref, dz_ref):
    f32 = jnp.float32
    units = [(pw, ph) for pw in range(2) for ph in range(2)]
    totals = []

    def multiply(pw, ph):
        y_ref[2 * pw + ph] = jnp.dot(
            xs_ref[pw],
            wz_ref[pw, :, ph * 256 : ph * 256 + 256],
            preferred_element_type=f32,
        )

    def finish(pw, ph):
        for h in range(4):
            half = 0.5 * bias_ref[...]
            for a in range(2):
                s = h + a + ph - 1
                if 0 <= s < 4:
                    half = half + y_ref[
                        2 * pw + ph, s * 144 : s * 144 + 144, a * 128 : a * 128 + 128
                    ]
            t = jnp.tanh(half)
            lines = slice(h * 144, h * 144 + 144)
            dz = cp_ref[2 * ph + pw, lines] * (1.0 + t) * (1.0 + half * (1.0 - t))
            dz = dz.astype(jnp.bfloat16)
            totals.append(jnp.sum(dz.astype(f32), axis=0, keepdims=True))
            for a in range(2):
                s = h + a + ph - 1
                if 0 <= s < 4:
                    col = ph * 256 + a * 128
                    dz_ref[pw, s * 144 : s * 144 + 144, col : col + 128] = dz

    multiply(*units[0])
    for step in range(4):
        if step < 3:
            multiply(*units[step + 1])
        finish(*units[step])
    return sum(totals)


def clear_edges(dz_ref):
    zero = jnp.zeros((144, 128), jnp.bfloat16)
    for pw in range(2):
        dz_ref[pw, 432:576, 0:128] = zero
        dz_ref[pw, 0:144, 384:512] = zero


def backward(xt_ref, part, dz_ref, g_ref, k):
    for pw in range(2):
        g_ref[k, pw] = jnp.dot(
            xt_ref[part, pw], dz_ref[pw], preferred_element_type=jnp.float32
        )


def tap_sums(g_ref, k, base, store):
    for kd in range(3):
        line = {}
        for pw in range(2):
            for b in range(2):
                row = pl.multiple_of(kd * 64 + b * 32 + base, 16)
                part = [
                    g_ref[k, pw, pl.ds(row, 16), c * 128 : c * 128 + 128]
                    for c in range(4)
                ]
                for kh in range(3):
                    line[pw, b, kh] = part[OFFSET[0][kh]] + part[2 + OFFSET[1][kh]]
        for kh in range(3):
            for kw in range(3):
                store(
                    9 * kd + 3 * kh + kw,
                    line[0, OFFSET[0][kw], kh] + line[1, OFFSET[1][kw], kh],
                )


def whole_kernel(
    scale, counts_any, w_any, x_any, cot_any, bias_any, o_any, b_ref,
    counts_ref, w_raw, w_pair, x_raw, cot_raw, bias_ref,
    wf_ref, f_ref, cf_ref, cp_ref, xs_ref, xt_ref, wz_ref, y_ref, dz_ref, g_ref,
    w_all, parts, sx, rx, s1, r1, s2, r2, keep, s3, r3, last, sb, rb,
    fetch, sw3, rw3, sw1, rw1, sw2, rw2, ss1, rs1, ss2, rs2, ss3, rs3, ss4, rs4, ssb, rsb, ssx, rsx, ready,
):
    grp = lax.axis_index("grp")
    dev = lax.axis_index("dev")
    depth = dev // 2
    core = dev % 2
    f32, bf16 = jnp.float32, jnp.bfloat16
    masks = (3, 2, 1)
    pair = {"dev": depth * 2 + (1 - core)}
    across = [{"grp": xor(grp, m)} for m in masks]
    along = [{"dev": xor(depth, m) * 2 + core} for m in masks]
    cross = [{"grp": xor(grp, m), "dev": depth * 2 + (1 - core)} for m in masks]

    barrier = pltpu.get_barrier_semaphore()
    for peer in along + across:
        pl.semaphore_signal(barrier, inc=1, device_id=peer, device_id_type=MESH)

    @pl.when(core == 0)
    def _():
        for peer in cross + [pair]:
            pl.semaphore_signal(barrier, inc=1, device_id=peer, device_id_type=MESH)

    fetches = []
    for i, (src, dst) in enumerate(
        (
            (w_any, w_raw),
            (cot_any, cot_raw),
            (x_any, x_raw),
            (bias_any, bias_ref),
            (counts_any, counts_ref),
        )
    ):
        fetches.append(pltpu.make_async_copy(src, dst, fetch.at[i]))
        fetches[i].start()

    def send(src, dst, ssem, rsem, peer):
        copy = pltpu.make_async_remote_copy(
            src_ref=src, dst_ref=dst, send_sem=ssem, recv_sem=rsem,
            device_id=peer, device_id_type=MESH,
        )
        copy.start()
        return copy

    pl.semaphore_wait(barrier, 6 + 4 * core)

    @pl.when(core == 1)
    def _():
        for peer in cross + [pair]:
            pl.semaphore_signal(ready, inc=1, device_id=peer, device_id_type=MESH)

    fetches[0].wait()
    quarter = w_raw.at[pl.ds(pl.multiple_of((7 * grp - grp // 3) * 16, 16), 112)]
    out = [
        send(quarter, w_all.at[dev, grp], sw1.at[k], rw1.at[k], along[k])
        for k in range(3)
    ]
    clear_edges(dz_ref)
    zero = jnp.zeros((16, 128), bf16)
    for k in range(4):
        s1[k, 27] = zero
        parts[k, 27] = jnp.zeros((16, 128), f32)
    for k in range(2):
        sx[k, 27] = zero
    wf_ref[0] = w_raw[...].astype(f32)
    combine_shard(wf_ref.at[0], dev, wz_ref)
    fetches[1].wait()
    fetches[4].wait()
    lay_out_cotangent(counts_ref[grp * 8 + dev], cot_raw, cf_ref, cp_ref)
    spread = {}
    for k in (2, 1, 0):
        out[k].wait_recv()
        block = w_all.at[xor(depth, masks[k]) * 2 + core, grp]
        for j in range(3):
            spread[k, j] = send(block, block, sw3.at[k, j], rw3.at[k, j], across[j])

    @pl.when(core == 0)
    def _():
        pl.semaphore_wait(ready, 4)

    swap = [send(w_raw, w_pair, sw2.at[3], rw2.at[3], pair)]
    fetches[2].wait()
    lay_out_tiles(x_raw, f_ref, xs_ref, xt_ref)
    swap[0].wait_recv()
    wf_ref[1] = w_pair[...].astype(f32)
    combine_shard(wf_ref.at[1], depth * 2 + 1 - core, wz_ref)
    for k in (2, 1, 0):
        for j in range(3):
            spread[k, j].wait_recv()
        block = w_all.at[xor(depth, masks[k]) * 2 + core]
        swap.append(send(block, block, sw2.at[k], rw2.at[k], pair))
        spread_rows(w_all, xor(depth, masks[k]) * 2 + core, wf_ref.at[0])
        combine_shard(wf_ref.at[0], xor(depth, masks[k]) * 2 + core, wz_ref)
    for i, k in enumerate((2, 1, 0)):
        swap[1 + i].wait_recv()
        spread_rows(w_all, xor(depth, masks[k]) * 2 + 1 - core, wf_ref.at[1])
        combine_shard(wf_ref.at[1], xor(depth, masks[k]) * 2 + 1 - core, wz_ref)
    fetches[3].wait()
    total_b = forward(xs_ref, wz_ref, y_ref, cp_ref, bias_ref, dz_ref)

    sb[0] = jnp.broadcast_to(total_b, (8, 128))
    bias_start = send(sb.at[0], rb.at[0], ssb.at[0], rsb.at[0], pair)
    for copy in out + list(spread.values()) + swap:
        copy.wait_send()

    def reduce_all(early):
        first, second, third = {}, {}, {}
        after = [1 - (depth - k + 2) // 3 for k in range(3)]
        goal = [k + after[k] for k in range(3)] + [depth]
        place = [depth - 1 + after[k] for k in range(3)]

        def work(k):
            backward(xt_ref, goal[k], dz_ref, g_ref, k)

        def give(k):
            def to_pair(tap, value):
                s1[k, tap] = value.astype(bf16)

            tap_sums(g_ref, k, 16 if early else 0, to_pair)
            first[k] = send(s1.at[k], r1.at[k], ss1.at[k], rs1.at[k], pair)

        def own(k):
            def to_self(tap, value):
                parts[k, tap] = value

            tap_sums(g_ref, k, 0 if early else 16, to_self)

        def start_second(k):
            arrived = pltpu.make_async_remote_copy(
                src_ref=s1.at[k], dst_ref=r1.at[k], send_sem=ss1.at[k], recv_sem=rs1.at[k],
                device_id=pair, device_id_type=MESH,
            )
            arrived.wait_recv()
            for j in range(4):
                owner = xor(grp, masks[j]) if j < 3 else grp
                taps = pl.ds(owner * 7, 7)
                total = parts[k, taps] + r1[k, taps].astype(f32)
                if j < 3:
                    s2[k, j] = total.astype(bf16)
                    second[k, j] = send(
                        s2.at[k, j], r2.at[k, j], ss2.at[k, j], rs2.at[k, j], across[j]
                    )
                else:
                    keep[k] = total

        direct = {}

        def send_direct(block):
            mine = block == (0 if early else 1)

            def stage(tap, value):
                sx[block, tap] = value.astype(bf16)
                if mine:
                    parts[0, tap] = value

            tap_sums(g_ref, 0, 16 * block, stage)
            for j in range(3):
                slot = j if mine else 3 + j
                taps = pl.ds(xor(grp, masks[j]) * 7, 7)
                direct[slot] = send(
                    sx.at[block, taps], rx.at[slot], ssx.at[slot], rsx.at[slot],
                    across[j] if mine else cross[j],
                )
            if not mine:
                direct[6] = send(
                    sx.at[block, pl.ds(grp * 7, 7)], rx.at[6], ssx.at[6], rsx.at[6], pair
                )

        def start_third(k):
            if k == 0:
                total = parts[0, pl.ds(grp * 7, 7)]
                for i in (6, 0, 1, 2, 3, 4, 5):
                    direct[i].wait_recv()
                    total += rx[i].astype(f32)
            else:
                total = keep[k]
                for j in range(3):
                    second[k, j].wait_recv()
                    total += r2[k, j].astype(f32)
            if k < 3:
                s3[k] = total.astype(bf16)
                third[k] = send(
                    s3.at[k], r3.at[place[k]], ss3.at[k], rs3.at[place[k]],
                    {"dev": goal[k] * 2 + core},
                )
            else:
                keep[k] = total

        bias_copies = []

        def bias_across():
            bias_start.wait_recv()
            sb[1] = sb[0] + rb[0]
            for k in range(3):
                bias_copies.append(
                    send(sb.at[1], rb.at[1 + k], ssb.at[1 + k], rsb.at[1 + k], across[k])
                )

        def bias_along():
            for k in range(3):
                bias_copies[k].wait_recv()
            sb[2] = (sb[1] + rb[3]) + (rb[2] + rb[1])
            for k in range(3):
                bias_copies.append(
                    send(sb.at[2], rb.at[4 + k], ssb.at[4 + k], rsb.at[4 + k], along[k])
                )

        if early:
            work(0)
            send_direct(0)
            work(1)
            own(1)
            bias_across()
            work(2)
            own(2)
            send_direct(1)
            start_second(1)
            work(3)
            own(3)
            start_second(2)
            give(1)
            start_second(3)
            give(2)
            give(3)
        else:
            work(0)
            send_direct(0)
            work(1)
            give(1)
            bias_across()
            work(2)
            give(2)
            send_direct(1)
            work(3)
            give(3)
            own(1)
            start_second(1)
            own(2)
            start_second(2)
            own(3)
            start_second(3)
        start_third(0)
        bias_along()
        start_third(1)
        start_third(2)
        start_third(3)
        total = keep[3]
        for k in range(3):
            pltpu.make_async_remote_copy(
                src_ref=s3.at[k], dst_ref=r3.at[k], send_sem=ss3.at[k], recv_sem=rs3.at[k],
                device_id=along[k], device_id_type=MESH,
            ).wait_recv()
            total += r3[k].astype(f32)
        last[...] = (total * scale).astype(bf16)
        fourth = [
            send(last, o_any.at[grp], ss4.at[k], rs4.at[k], across[k]) for k in range(3)
        ]
        mine = pltpu.make_async_copy(last, o_any.at[grp], fetch.at[5])
        mine.start()
        for k in range(3):
            bias_copies[3 + k].wait_recv()
        whole_b = (((sb[2] + rb[6]) + (rb[5] + rb[4])) * scale)[0:1]
        share = jnp.zeros((1, 16), f32)
        for d in range(8):
            share = jnp.where(dev == d, whole_b[:, d * 16 : d * 16 + 16], share)
        b_ref[...] = share
        for copy in list(direct.values()) + list(first.values()) + list(second.values()) + list(third.values()):
            copy.wait_send()
        for copy in [bias_start] + bias_copies + fourth:
            copy.wait_send()
        mine.wait()
        for k in (2, 1, 0):
            fourth[k].wait_recv()

    @pl.when(core == 0)
    def _():
        reduce_all(True)

    @pl.when(core == 1)
    def _():
        reduce_all(False)


def whole(counts, w, x, cot, bias, scale):
    bf16, f32 = jnp.bfloat16, jnp.float32
    sem = pltpu.SemaphoreType.DMA
    vmem = pltpu.VMEM
    return pl.pallas_call(
        functools.partial(whole_kernel, scale),
        out_shape=(
            jax.ShapeDtypeStruct((4, 7, 16, 128), bf16),
            jax.ShapeDtypeStruct((1, 16), f32),
        ),
        in_specs=[pl.BlockSpec(memory_space=pltpu.HBM)] * 5,
        out_specs=[
            pl.BlockSpec(memory_space=pltpu.VMEM),
            pl.BlockSpec(memory_space=pltpu.VMEM),
        ],
        scratch_shapes=[
            pltpu.SMEM((32,), jnp.int32),
            vmem((432, 128), bf16),
            vmem((432, 128), bf16),
            vmem((576, 128), bf16),
            vmem((2304, 128), bf16),
            vmem((1, 128), f32),
            vmem((2, 432, 128), f32),
            vmem((3, 592, 128), f32),
            vmem((8, 288, 128), f32),
            vmem((4, 576, 128), f32),
            vmem((2, 576, 768), bf16),
            vmem((4, 2, 192, 576), bf16),
            vmem((2, 768, 512), bf16),
            vmem((4, 576, 256), f32),
            vmem((2, 576, 512), bf16),
            vmem((4, 2, 192, 512), f32),
            vmem((8, 4, 112, 128), bf16),
            vmem((4, 28, 16, 128), f32),
            vmem((2, 28, 16, 128), bf16),
            vmem((7, 7, 16, 128), bf16),
            vmem((4, 28, 16, 128), bf16),
            vmem((4, 28, 16, 128), bf16),
            vmem((4, 3, 7, 16, 128), bf16),
            vmem((4, 3, 7, 16, 128), bf16),
            vmem((4, 7, 16, 128), f32),
            vmem((3, 7, 16, 128), bf16),
            vmem((3, 7, 16, 128), bf16),
            vmem((7, 16, 128), bf16),
            vmem((3, 8, 128), f32),
            vmem((7, 8, 128), f32),
            sem((6,)), sem((3, 3)), sem((3, 3)),
            sem((3,)), sem((3,)), sem((4,)), sem((4,)),
            sem((4,)), sem((4,)), sem((4, 3)), sem((4, 3)),
            sem((3,)), sem((3,)), sem((3,)), sem((3,)),
            sem((7,)), sem((7,)), sem((7,)), sem((7,)), pltpu.SemaphoreType.REGULAR,
        ],
        compiler_params=pltpu.CompilerParams(
            collective_id=1, has_side_effects=True, vmem_limit_bytes=48 * 2**20
        ),
    )(*(pltpu.with_memory_space_constraint(v, pltpu.HBM) for v in (counts, w, x, cot, bias)))


def sort_rows_kernel(w_ref, b_ref, o_any, p_any, rows_ref, sems):
    bias = pltpu.make_async_copy(b_ref, p_any, sems.at[1])
    bias.start()
    for k in range(27):
        rows_ref[pl.ds(k, 16, 27), :] = w_ref[k // 7, k % 7].astype(jnp.float32)
    copy = pltpu.make_async_copy(rows_ref, o_any, sems.at[0])
    copy.start()
    bias.wait()
    copy.wait()


def sort_rows(part_w, part_b):
    f32 = jnp.float32
    return pl.pallas_call(
        sort_rows_kernel,
        out_shape=(
            jax.ShapeDtypeStruct((432, 128), f32),
            jax.ShapeDtypeStruct(part_b.shape, f32),
        ),
        in_specs=[pl.BlockSpec(memory_space=pltpu.VMEM)] * 2,
        out_specs=[pl.BlockSpec(memory_space=pltpu.HBM)] * 2,
        scratch_shapes=[pltpu.VMEM((432, 128), f32), pltpu.SemaphoreType.DMA((2,))],
        compiler_params=pltpu.CompilerParams(vmem_limit_bytes=4 * 2**20),
    )(part_w, part_b)


def body(tiles, cotangent, weight, bias, counts):
    num_dev = lax.axis_size("dev")
    num_grp = lax.axis_size("grp")
    cap, frames, hl, wl, cin = tiles.shape
    cout = weight.shape[1]
    my_dev = lax.axis_index("dev")
    my_grp = lax.axis_index("grp")
    scale = 1.0 / math.sqrt(cap * num_dev * num_grp * frames * 4 * hl * wl)
    bias = bias.reshape(1, cout)
    if (num_grp, num_dev) == (4, 8):
        x = tiles.reshape(cap * frames * hl * wl, cin)
        cot = cotangent.reshape(cap * frames * 4 * hl * wl, cout)
        part_w, part_b = sort_rows(*whole(counts, weight, x, cot, bias, scale))
        return part_w, part_b.reshape(cout // num_dev)

    mine = weight.reshape(cin // num_dev, 27, cout).transpose(1, 0, 2)
    x = tiles.transpose(2, 3, 0, 1, 4).reshape(hl * wl * cap * frames, cin)
    cot = cotangent.reshape(cap, frames, hl, 2, wl, 2, cout).transpose(3, 5, 2, 4, 0, 1, 6)
    cot = cot.reshape(4, hl * wl * cap * frames, cout)
    share = cout // num_dev
    gathered = lax.all_gather(mine, "dev", axis=0, tiled=False)
    if num_dev != 8:
        gathered = gathered.transpose(1, 0, 2, 3).reshape(27, 8, 16, cout)
        gathered = gathered.transpose(1, 0, 2, 3)
    count = lax.dynamic_slice_in_dim(counts, my_grp * num_dev + my_dev, 1)
    parts = terms(count, gathered, x, cot, bias)
    flat = parts[:, :27].transpose(0, 2, 1, 3).reshape(cin * 27, cout)
    part_w = lax.psum_scatter(flat, "dev", scatter_dimension=0, tiled=True)
    part_w = lax.psum(part_w, "grp")
    total_b = lax.psum(parts[0, 27, 0], ("grp", "dev"))
    part_b = lax.dynamic_slice_in_dim(total_b, my_dev * share, share, 0)
    return part_w * scale, part_b * scale


def solution(mesh):
    return jax.shard_map(
        body,
        mesh=mesh,
        in_specs=(
            P(("grp", "dev"), None, None, None, None),
            P(("grp", "dev"), None, None, None, None),
            P("dev", None),
            P(),
            P(),
        ),
        out_specs=(P("dev", None), P("dev")),
        check_vma=False,
    )
```

```python
import functools
import math

import jax
import jax.numpy as jnp
from jax import lax
from jax.experimental import pallas as pl
from jax.experimental.pallas import tpu as pltpu
from jax.sharding import PartitionSpec as P

MESH = pl.DeviceIdType.MESH
TAPS = {(0, 0): (0,), (0, 1): (1, 2), (1, 0): (0, 1), (1, 1): (2,)}
OFFSET = ((0, 1, 1), (0, 0, 1))


def build_windows(x_ref, f_ref, xs_ref):
    rows = x_ref.shape[0]
    slab = rows // 4
    pad = 40
    row = lax.broadcasted_iota(jnp.int32, (rows, 128), 0).astype(jnp.float32)
    frame = row - 9.0 * jnp.floor((row + 0.5) * (1.0 / 9.0))
    place = lax.broadcasted_iota(jnp.int32, (slab, 128), 0)
    xs_ref[0:slab] = jnp.zeros((slab, 1152), jnp.bfloat16)
    xs_ref[5 * slab : 6 * slab] = jnp.zeros((slab, 1152), jnp.bfloat16)
    f_ref[...] = jnp.zeros_like(f_ref)
    now = x_ref[...].astype(jnp.float32)
    f_ref[2, pad : pad + rows] = now
    back1 = jnp.where(frame < 0.5, now, f_ref[2, pad - 1 : pad - 1 + rows])
    f_ref[1, pad : pad + rows] = back1
    f_ref[0, pad : pad + rows] = jnp.where(
        frame < 1.5, back1, f_ref[2, pad - 2 : pad - 2 + rows]
    )
    for h in range(4):
        for dw in range(3):
            for kd in range(3):
                start = pad + h * slab + (dw - 1) * 36
                piece = f_ref[kd, start : start + slab]
                if dw == 0:
                    piece = jnp.where(place < 36, 0.0, piece)
                if dw == 2:
                    piece = jnp.where(place >= slab - 36, 0.0, piece)
                col = dw * 384 + kd * 128
                xs_ref[(h + 1) * slab : (h + 2) * slab, col : col + 128] = piece.astype(
                    jnp.bfloat16
                )


def combine_weights(w_ref, wz_ref):
    chans = 128
    for kd in range(3):
        tap = {}
        for kh in range(3):
            for kw in range(3):
                piece = w_ref[:, 9 * kd + 3 * kh + kw]
                tap[kh, kw] = piece.reshape(chans, chans).astype(jnp.float32)
        for ph in range(2):
            for a in range(2):
                line = [sum(tap[kh, kw] for kh in TAPS[ph, a]) for kw in range(3)]
                for pw in range(2):
                    for b in range(2):
                        both = sum(line[kw] for kw in TAPS[pw, b])
                        row = (b + pw) * 384 + kd * 128
                        col = (2 * ph + pw) * 128
                        wz_ref[a + ph, row : row + 128, col : col + 128] = both.astype(
                            jnp.bfloat16
                        )


def products(count, xs_ref, cot_ref, bias_ref, wz_ref, g_ref):
    slab = xs_ref.shape[0] // 6
    rows = 4 * slab
    row = lax.broadcasted_iota(jnp.int32, (rows, 128), 0).astype(jnp.float32)
    place = row - 36.0 * jnp.floor((row + 0.5) * (1.0 / 36.0))
    live = place < 9.0 * count.astype(jnp.float32)
    cols = ((0, 256), (0, 512), (256, 256))

    def window(dh):
        return xs_ref[dh * slab : dh * slab + rows, :]

    mid = jnp.dot(window(1), wz_ref[1], preferred_element_type=jnp.float32)
    top = jnp.dot(window(0), wz_ref[0, :, 0:256], preferred_element_type=jnp.float32)
    low = jnp.dot(window(2), wz_ref[2, :, 256:512], preferred_element_type=jnp.float32)
    parts = []
    total_b = jnp.zeros((1, 128), jnp.float32)
    for p in range(4):
        side = (top if p < 2 else low)[:, (p % 2) * 128 : (p % 2) * 128 + 128]
        z = mid[:, p * 128 : p * 128 + 128] + side + bias_ref[...]
        sig = jax.nn.sigmoid(z)
        dz = cot_ref[p].astype(jnp.float32) * sig * (1.0 + z * (1.0 - sig))
        dz = jnp.where(live, dz, 0.0).astype(jnp.bfloat16)
        total_b += jnp.sum(dz.astype(jnp.float32), axis=0, keepdims=True)
        parts.append(dz)
    dz = jnp.concatenate(parts, axis=1)
    for dh in range(3):
        start, width = cols[dh]
        g_ref[dh, :, start : start + width] = lax.dot_general(
            window(dh),
            dz[:, start : start + width],
            (((0,), (0,)), ((), ())),
            preferred_element_type=jnp.float32,
        )
    return total_b


def tap_gradient(g_ref, k, base=0, size=128):
    kd, kh, kw = k // 9, k // 3 % 3, k % 3
    total = None
    for ph in range(2):
        for pw in range(2):
            row = (OFFSET[pw][kw] + pw) * 384 + kd * 128
            col = (2 * ph + pw) * 128
            term = g_ref[
                OFFSET[ph][kh] + ph, pl.ds(base + row, size), col : col + 128
            ]
            total = term if total is None else total + term
    return total


WORK = [
    pltpu.VMEM((3, 656, 128), jnp.float32),
    pltpu.VMEM((864, 1152), jnp.bfloat16),
    pltpu.VMEM((3, 1152, 512), jnp.bfloat16),
    pltpu.VMEM((3, 1152, 512), jnp.float32),
]


def terms_kernel(
    count_ref, w_ref, x_ref, cot_ref, bias_ref, out_ref, f_ref, xs_ref, wz_ref, g_ref
):
    build_windows(x_ref, f_ref, xs_ref)
    wz_ref[...] = jnp.zeros_like(wz_ref)
    combine_weights(w_ref, wz_ref)
    total_b = products(count_ref[0], xs_ref, cot_ref, bias_ref, wz_ref, g_ref)
    for k in range(27):
        out_ref[:, k] = tap_gradient(g_ref, k).reshape(8, 16, 128)
    out_ref[:, 27] = jnp.broadcast_to(total_b.reshape(1, 1, 128), (8, 16, 128))


def terms(count, w, x, cot, bias):
    return pl.pallas_call(
        terms_kernel,
        out_shape=jax.ShapeDtypeStruct((8, 28, 16, 128), jnp.float32),
        in_specs=[pl.BlockSpec(memory_space=pltpu.SMEM)]
        + [pl.BlockSpec(memory_space=pltpu.VMEM)] * 4,
        out_specs=pl.BlockSpec(memory_space=pltpu.VMEM),
        scratch_shapes=WORK,
        compiler_params=pltpu.CompilerParams(vmem_limit_bytes=48 * 2**20),
    )(count, w, x, cot, bias)


def xor(value, mask):
    if mask == 1:
        return value + 1 - 2 * (value % 2)
    if mask == 2:
        return (value + 2) % 4
    return 3 - value


def lay_out_tiles(x_raw, f_ref, xs_ref, xt_ref):
    pad = 8
    rows = 576
    full = x_raw[...].astype(jnp.float32)
    for tf in range(36):
        for h in range(4):
            at = pad + h * 144 + tf * 4
            f_ref[2, at : at + 4] = full[tf * 16 + h * 4 : tf * 16 + h * 4 + 4]
    row = lax.broadcasted_iota(jnp.int32, (144, 128), 0)
    w = row % 4
    frame = (row // 4) % 9
    for h in range(4):
        at = pad + h * 144
        now = f_ref[2, at : at + 144]
        back1 = jnp.where(frame < 1, now, f_ref[2, at - 4 : at + 140])
        back2 = jnp.where(frame < 2, back1, f_ref[2, at - 8 : at + 136])
        f_ref[1, at : at + 144] = back1
        f_ref[0, at : at + 144] = back2
    for kd in range(3):
        for h in range(4):
            at = pad + h * 144
            lines = slice(h * 144, h * 144 + 144)
            left = jnp.where(w == 0, 0.0, f_ref[kd, at - 1 : at + 143])
            here = f_ref[kd, at : at + 144]
            right = jnp.where(w == 3, 0.0, f_ref[kd, at + 1 : at + 145])
            left, here, right = (
                piece.astype(jnp.bfloat16) for piece in (left, here, right)
            )
            col = kd * 256
            xs_ref[0, lines, col : col + 128] = left
            xs_ref[0, lines, col + 128 : col + 256] = here
            xs_ref[1, lines, col : col + 128] = here
            xs_ref[1, lines, col + 128 : col + 256] = right
    for kd in range(3):
        for pw in range(2):
            for b in range(2):
                col = kd * 256 + b * 128
                if (pw, b) == (1, 0):
                    continue
                block = xs_ref[pw, :, col : col + 128].astype(jnp.float32).T
                block = block.astype(jnp.bfloat16)
                for part in range(4):
                    piece = block[part * 32 : part * 32 + 32]
                    at = kd * 64 + b * 32
                    xt_ref[part, pw, at : at + 32, :] = piece
                    if (pw, b) == (0, 1):
                        xt_ref[part, 1, kd * 64 : kd * 64 + 32, :] = piece


def lay_out_cotangent(count, cot_raw, cf_ref, cp_ref):
    live = lax.broadcasted_iota(jnp.int32, (144, 128), 0) < 36 * count
    for tf in range(36):
        full = cot_raw[tf * 64 : tf * 64 + 64].astype(jnp.float32)
        for line in range(8):
            cf_ref[line, tf * 8 : tf * 8 + 8] = full[line * 8 : line * 8 + 8]
    for h in range(4):
        for ph in range(2):
            for pw in range(2):
                here = cf_ref[2 * h + ph, pl.ds(pw, 144, 2), :]
                cp_ref[2 * ph + pw, h * 144 : h * 144 + 144] = jnp.where(
                    live, 0.5 * here, 0.0
                )


def spread_rows(w_ref, d, wf_ref):
    for q in range(4):
        at = (7 * q - q // 3) * 16
        wf_ref[at : at + 112] = w_ref[d, q].astype(jnp.float32)


def combine_shard(wf_ref, d, wz_ref):
    for kd in range(3):
        tap = {}
        for kh in range(3):
            for kw in range(3):
                tap[kh, kw] = 0.5 * wf_ref[pl.ds(9 * kd + 3 * kh + kw, 16, 27), :]
        for ph in range(2):
            for a in range(2):
                line = [sum(tap[kh, kw] for kh in TAPS[ph, a]) for kw in range(3)]
                for pw in range(2):
                    for b in range(2):
                        both = sum(line[kw] for kw in TAPS[pw, b])
                        row = pl.multiple_of(kd * 256 + b * 128 + d * 16, 16)
                        col = (2 * ph + a) * 128
                        wz_ref[pw, pl.ds(row, 16), col : col + 128] = both.astype(
                            jnp.bfloat16
                        )


def forward(xs_ref, wz_ref, y_ref, cp_ref, bias_ref, dz_ref):
    f32 = jnp.float32
    units = [(pw, ph) for pw in range(2) for ph in range(2)]
    totals = []

    def multiply(pw, ph):
        y_ref[2 * pw + ph] = jnp.dot(
            xs_ref[pw],
            wz_ref[pw, :, ph * 256 : ph * 256 + 256],
            preferred_element_type=f32,
        )

    def finish(pw, ph):
        for h in range(4):
            half = 0.5 * bias_ref[...]
            for a in range(2):
                s = h + a + ph - 1
                if 0 <= s < 4:
                    half = half + y_ref[
                        2 * pw + ph, s * 144 : s * 144 + 144, a * 128 : a * 128 + 128
                    ]
            t = jnp.tanh(half)
            lines = slice(h * 144, h * 144 + 144)
            dz = cp_ref[2 * ph + pw, lines] * (1.0 + t) * (1.0 + half * (1.0 - t))
            dz = dz.astype(jnp.bfloat16)
            totals.append(jnp.sum(dz.astype(f32), axis=0, keepdims=True))
            for a in range(2):
                s = h + a + ph - 1
                if 0 <= s < 4:
                    col = ph * 256 + a * 128
                    dz_ref[pw, s * 144 : s * 144 + 144, col : col + 128] = dz

    multiply(*units[0])
    for step in range(4):
        if step < 3:
            multiply(*units[step + 1])
        finish(*units[step])
    return sum(totals)


def clear_edges(dz_ref):
    zero = jnp.zeros((144, 128), jnp.bfloat16)
    for pw in range(2):
        dz_ref[pw, 432:576, 0:128] = zero
        dz_ref[pw, 0:144, 384:512] = zero


def backward(xt_ref, part, dz_ref, g_ref, k):
    for pw in range(2):
        g_ref[k, pw] = jnp.dot(
            xt_ref[part, pw], dz_ref[pw], preferred_element_type=jnp.float32
        )


def tap_sums(g_ref, k, base, store):
    for kd in range(3):
        line = {}
        for pw in range(2):
            for b in range(2):
                row = pl.multiple_of(kd * 64 + b * 32 + base, 16)
                part = [
                    g_ref[k, pw, pl.ds(row, 16), c * 128 : c * 128 + 128]
                    for c in range(4)
                ]
                for kh in range(3):
                    line[pw, b, kh] = part[OFFSET[0][kh]] + part[2 + OFFSET[1][kh]]
        for kh in range(3):
            for kw in range(3):
                store(
                    9 * kd + 3 * kh + kw,
                    line[0, OFFSET[0][kw], kh] + line[1, OFFSET[1][kw], kh],
                )


def whole_kernel(
    scale, counts_any, w_any, x_any, cot_any, bias_any, o_any, b_ref,
    counts_ref, w_raw, w_pair, x_raw, cot_raw, bias_ref,
    wf_ref, f_ref, cf_ref, cp_ref, xs_ref, xt_ref, wz_ref, y_ref, dz_ref, g_ref,
    w_all, parts, sx, rx, s1, r1, s2, r2, keep, s3, r3, last, sb, rb,
    fetch, sw3, rw3, sw1, rw1, sw2, rw2, ss1, rs1, ss2, rs2, ss3, rs3, ss4, rs4, ssb, rsb, ssx, rsx, ready,
):
    grp = lax.axis_index("grp")
    dev = lax.axis_index("dev")
    depth = dev // 2
    core = dev % 2
    f32, bf16 = jnp.float32, jnp.bfloat16
    masks = (3, 2, 1)
    pair = {"dev": depth * 2 + (1 - core)}
    across = [{"grp": xor(grp, m)} for m in masks]
    along = [{"dev": xor(depth, m) * 2 + core} for m in masks]
    cross = [{"grp": xor(grp, m), "dev": depth * 2 + (1 - core)} for m in masks]

    barrier = pltpu.get_barrier_semaphore()
    for peer in along + across:
        pl.semaphore_signal(barrier, inc=1, device_id=peer, device_id_type=MESH)

    @pl.when(core == 0)
    def _():
        for peer in cross + [pair]:
            pl.semaphore_signal(barrier, inc=1, device_id=peer, device_id_type=MESH)

    fetches = []
    for i, (src, dst) in enumerate(
        (
            (w_any, w_raw),
            (cot_any, cot_raw),
            (x_any, x_raw),
            (bias_any, bias_ref),
            (counts_any, counts_ref),
        )
    ):
        fetches.append(pltpu.make_async_copy(src, dst, fetch.at[i]))
        fetches[i].start()

    def send(src, dst, ssem, rsem, peer):
        copy = pltpu.make_async_remote_copy(
            src_ref=src, dst_ref=dst, send_sem=ssem, recv_sem=rsem,
            device_id=peer, device_id_type=MESH,
        )
        copy.start()
        return copy

    pl.semaphore_wait(barrier, 6 + 4 * core)

    @pl.when(core == 1)
    def _():
        for peer in cross + [pair]:
            pl.semaphore_signal(ready, inc=1, device_id=peer, device_id_type=MESH)

    fetches[0].wait()
    quarter = w_raw.at[pl.ds(pl.multiple_of((7 * grp - grp // 3) * 16, 16), 112)]
    out = [
        send(quarter, w_all.at[dev, grp], sw1.at[k], rw1.at[k], along[k])
        for k in range(3)
    ]
    clear_edges(dz_ref)
    zero = jnp.zeros((16, 128), bf16)
    for k in range(4):
        s1[k, 27] = zero
        parts[k, 27] = jnp.zeros((16, 128), f32)
    for k in range(2):
        sx[k, 27] = zero
    wf_ref[0] = w_raw[...].astype(f32)
    combine_shard(wf_ref.at[0], dev, wz_ref)
    fetches[1].wait()
    fetches[4].wait()
    lay_out_cotangent(counts_ref[grp * 8 + dev], cot_raw, cf_ref, cp_ref)
    spread = {}
    for k in (2, 1, 0):
        out[k].wait_recv()
        block = w_all.at[xor(depth, masks[k]) * 2 + core, grp]
        for j in range(3):
            spread[k, j] = send(block, block, sw3.at[k, j], rw3.at[k, j], across[j])

    @pl.when(core == 0)
    def _():
        pl.semaphore_wait(ready, 4)

    swap = [send(w_raw, w_pair, sw2.at[3], rw2.at[3], pair)]
    fetches[2].wait()
    lay_out_tiles(x_raw, f_ref, xs_ref, xt_ref)
    swap[0].wait_recv()
    wf_ref[1] = w_pair[...].astype(f32)
    combine_shard(wf_ref.at[1], depth * 2 + 1 - core, wz_ref)
    for k in (2, 1, 0):
        for j in range(3):
            spread[k, j].wait_recv()
        block = w_all.at[xor(depth, masks[k]) * 2 + core]
        swap.append(send(block, block, sw2.at[k], rw2.at[k], pair))
        spread_rows(w_all, xor(depth, masks[k]) * 2 + core, wf_ref.at[0])
        combine_shard(wf_ref.at[0], xor(depth, masks[k]) * 2 + core, wz_ref)
    for i, k in enumerate((2, 1, 0)):
        swap[1 + i].wait_recv()
        spread_rows(w_all, xor(depth, masks[k]) * 2 + 1 - core, wf_ref.at[1])
        combine_shard(wf_ref.at[1], xor(depth, masks[k]) * 2 + 1 - core, wz_ref)
    fetches[3].wait()
    total_b = forward(xs_ref, wz_ref, y_ref, cp_ref, bias_ref, dz_ref)

    sb[0] = jnp.broadcast_to(total_b, (8, 128))
    bias_start = send(sb.at[0], rb.at[0], ssb.at[0], rsb.at[0], pair)
    for copy in out + list(spread.values()) + swap:
        copy.wait_send()

    def reduce_all(early):
        first, second, third = {}, {}, {}
        after = [1 - (depth - k + 2) // 3 for k in range(3)]
        goal = [k + after[k] for k in range(3)] + [depth]
        place = [depth - 1 + after[k] for k in range(3)]

        def work(k):
            backward(xt_ref, goal[k], dz_ref, g_ref, k)

        def give(k):
            def to_pair(tap, value):
                s1[k, tap] = value.astype(bf16)

            tap_sums(g_ref, k, 16 if early else 0, to_pair)
            first[k] = send(s1.at[k], r1.at[k], ss1.at[k], rs1.at[k], pair)

        def own(k):
            def to_self(tap, value):
                parts[k, tap] = value

            tap_sums(g_ref, k, 0 if early else 16, to_self)

        def start_second(k):
            arrived = pltpu.make_async_remote_copy(
                src_ref=s1.at[k], dst_ref=r1.at[k], send_sem=ss1.at[k], recv_sem=rs1.at[k],
                device_id=pair, device_id_type=MESH,
            )
            arrived.wait_recv()
            for j in range(4):
                owner = xor(grp, masks[j]) if j < 3 else grp
                taps = pl.ds(owner * 7, 7)
                total = parts[k, taps] + r1[k, taps].astype(f32)
                if j < 3:
                    s2[k, j] = total.astype(bf16)
                    second[k, j] = send(
                        s2.at[k, j], r2.at[k, j], ss2.at[k, j], rs2.at[k, j], across[j]
                    )
                else:
                    keep[k] = total

        direct = {}

        def send_direct(block):
            mine = block == (0 if early else 1)

            def stage(tap, value):
                sx[block, tap] = value.astype(bf16)
                if mine:
                    parts[0, tap] = value

            tap_sums(g_ref, 0, 16 * block, stage)
            for j in range(3):
                slot = j if mine else 3 + j
                taps = pl.ds(xor(grp, masks[j]) * 7, 7)
                direct[slot] = send(
                    sx.at[block, taps], rx.at[slot], ssx.at[slot], rsx.at[slot],
                    across[j] if mine else cross[j],
                )
            if not mine:
                direct[6] = send(
                    sx.at[block, pl.ds(grp * 7, 7)], rx.at[6], ssx.at[6], rsx.at[6], pair
                )

        def start_third(k):
            if k == 0:
                total = parts[0, pl.ds(grp * 7, 7)]
                for i in (6, 0, 1, 2, 3, 4, 5):
                    direct[i].wait_recv()
                    total += rx[i].astype(f32)
            else:
                total = keep[k]
                for j in range(3):
                    second[k, j].wait_recv()
                    total += r2[k, j].astype(f32)
            if k < 3:
                s3[k] = total.astype(bf16)
                third[k] = send(
                    s3.at[k], r3.at[place[k]], ss3.at[k], rs3.at[place[k]],
                    {"dev": goal[k] * 2 + core},
                )
            else:
                keep[k] = total

        bias_copies = []

        def bias_across():
            bias_start.wait_recv()
            sb[1] = sb[0] + rb[0]
            for k in range(3):
                bias_copies.append(
                    send(sb.at[1], rb.at[1 + k], ssb.at[1 + k], rsb.at[1 + k], across[k])
                )

        def bias_along():
            for k in range(3):
                bias_copies[k].wait_recv()
            sb[2] = (sb[1] + rb[3]) + (rb[2] + rb[1])
            for k in range(3):
                bias_copies.append(
                    send(sb.at[2], rb.at[4 + k], ssb.at[4 + k], rsb.at[4 + k], along[k])
                )

        if early:
            work(0)
            send_direct(0)
            work(1)
            bias_across()
            own(1)
            work(2)
            own(2)
            send_direct(1)
            start_second(1)
            work(3)
            own(3)
            start_second(2)
            give(1)
            start_second(3)
            give(2)
            give(3)
        else:
            work(0)
            send_direct(0)
            work(1)
            give(1)
            bias_across()
            work(2)
            give(2)
            send_direct(1)
            work(3)
            give(3)
            own(1)
            start_second(1)
            own(2)
            start_second(2)
            own(3)
            start_second(3)
        start_third(0)
        bias_along()
        start_third(1)
        start_third(2)
        start_third(3)
        total = keep[3]
        for k in range(3):
            pltpu.make_async_remote_copy(
                src_ref=s3.at[k], dst_ref=r3.at[k], send_sem=ss3.at[k], recv_sem=rs3.at[k],
                device_id=along[k], device_id_type=MESH,
            ).wait_recv()
            total += r3[k].astype(f32)
        last[...] = (total * scale).astype(bf16)
        fourth = [
            send(last, o_any.at[grp], ss4.at[k], rs4.at[k], across[k]) for k in range(3)
        ]
        mine = pltpu.make_async_copy(last, o_any.at[grp], fetch.at[5])
        mine.start()
        for k in range(3):
            bias_copies[3 + k].wait_recv()
        whole_b = (((sb[2] + rb[6]) + (rb[5] + rb[4])) * scale)[0:1]
        share = jnp.zeros((1, 16), f32)
        for d in range(8):
            share = jnp.where(dev == d, whole_b[:, d * 16 : d * 16 + 16], share)
        b_ref[...] = share
        for copy in list(direct.values()) + list(first.values()) + list(second.values()) + list(third.values()):
            copy.wait_send()
        for copy in [bias_start] + bias_copies + fourth:
            copy.wait_send()
        mine.wait()
        for k in (2, 1, 0):
            fourth[k].wait_recv()

    @pl.when(core == 0)
    def _():
        reduce_all(True)

    @pl.when(core == 1)
    def _():
        reduce_all(False)


def whole(counts, w, x, cot, bias, scale):
    bf16, f32 = jnp.bfloat16, jnp.float32
    sem = pltpu.SemaphoreType.DMA
    vmem = pltpu.VMEM
    return pl.pallas_call(
        functools.partial(whole_kernel, scale),
        out_shape=(
            jax.ShapeDtypeStruct((4, 7, 16, 128), bf16),
            jax.ShapeDtypeStruct((1, 16), f32),
        ),
        in_specs=[pl.BlockSpec(memory_space=pltpu.HBM)] * 5,
        out_specs=[
            pl.BlockSpec(memory_space=pltpu.VMEM),
            pl.BlockSpec(memory_space=pltpu.VMEM),
        ],
        scratch_shapes=[
            pltpu.SMEM((32,), jnp.int32),
            vmem((432, 128), bf16),
            vmem((432, 128), bf16),
            vmem((576, 128), bf16),
            vmem((2304, 128), bf16),
            vmem((1, 128), f32),
            vmem((2, 432, 128), f32),
            vmem((3, 592, 128), f32),
            vmem((8, 288, 128), f32),
            vmem((4, 576, 128), f32),
            vmem((2, 576, 768), bf16),
            vmem((4, 2, 192, 576), bf16),
            vmem((2, 768, 512), bf16),
            vmem((4, 576, 256), f32),
            vmem((2, 576, 512), bf16),
            vmem((4, 2, 192, 512), f32),
            vmem((8, 4, 112, 128), bf16),
            vmem((4, 28, 16, 128), f32),
            vmem((2, 28, 16, 128), bf16),
            vmem((7, 7, 16, 128), bf16),
            vmem((4, 28, 16, 128), bf16),
            vmem((4, 28, 16, 128), bf16),
            vmem((4, 3, 7, 16, 128), bf16),
            vmem((4, 3, 7, 16, 128), bf16),
            vmem((4, 7, 16, 128), f32),
            vmem((3, 7, 16, 128), bf16),
            vmem((3, 7, 16, 128), bf16),
            vmem((7, 16, 128), bf16),
            vmem((3, 8, 128), f32),
            vmem((7, 8, 128), f32),
            sem((6,)), sem((3, 3)), sem((3, 3)),
            sem((3,)), sem((3,)), sem((4,)), sem((4,)),
            sem((4,)), sem((4,)), sem((4, 3)), sem((4, 3)),
            sem((3,)), sem((3,)), sem((3,)), sem((3,)),
            sem((7,)), sem((7,)), sem((7,)), sem((7,)), pltpu.SemaphoreType.REGULAR,
        ],
        compiler_params=pltpu.CompilerParams(
            collective_id=1, has_side_effects=True, vmem_limit_bytes=48 * 2**20
        ),
    )(*(pltpu.with_memory_space_constraint(v, pltpu.HBM) for v in (counts, w, x, cot, bias)))


def sort_rows_kernel(w_ref, b_ref, o_any, p_any, rows_ref, sems):
    bias = pltpu.make_async_copy(b_ref, p_any, sems.at[1])
    bias.start()
    for k in range(27):
        rows_ref[pl.ds(k, 16, 27), :] = w_ref[k // 7, k % 7].astype(jnp.float32)
    copy = pltpu.make_async_copy(rows_ref, o_any, sems.at[0])
    copy.start()
    bias.wait()
    copy.wait()


def sort_rows(part_w, part_b):
    f32 = jnp.float32
    return pl.pallas_call(
        sort_rows_kernel,
        out_shape=(
            jax.ShapeDtypeStruct((432, 128), f32),
            jax.ShapeDtypeStruct(part_b.shape, f32),
        ),
        in_specs=[pl.BlockSpec(memory_space=pltpu.VMEM)] * 2,
        out_specs=[pl.BlockSpec(memory_space=pltpu.HBM)] * 2,
        scratch_shapes=[pltpu.VMEM((432, 128), f32), pltpu.SemaphoreType.DMA((2,))],
        compiler_params=pltpu.CompilerParams(vmem_limit_bytes=4 * 2**20),
    )(part_w, part_b)


def body(tiles, cotangent, weight, bias, counts):
    num_dev = lax.axis_size("dev")
    num_grp = lax.axis_size("grp")
    cap, frames, hl, wl, cin = tiles.shape
    cout = weight.shape[1]
    my_dev = lax.axis_index("dev")
    my_grp = lax.axis_index("grp")
    scale = 1.0 / math.sqrt(cap * num_dev * num_grp * frames * 4 * hl * wl)
    bias = bias.reshape(1, cout)
    if (num_grp, num_dev) == (4, 8):
        x = tiles.reshape(cap * frames * hl * wl, cin)
        cot = cotangent.reshape(cap * frames * 4 * hl * wl, cout)
        part_w, part_b = sort_rows(*whole(counts, weight, x, cot, bias, scale))
        return part_w, part_b.reshape(cout // num_dev)

    mine = weight.reshape(cin // num_dev, 27, cout).transpose(1, 0, 2)
    x = tiles.transpose(2, 3, 0, 1, 4).reshape(hl * wl * cap * frames, cin)
    cot = cotangent.reshape(cap, frames, hl, 2, wl, 2, cout).transpose(3, 5, 2, 4, 0, 1, 6)
    cot = cot.reshape(4, hl * wl * cap * frames, cout)
    share = cout // num_dev
    gathered = lax.all_gather(mine, "dev", axis=0, tiled=False)
    if num_dev != 8:
        gathered = gathered.transpose(1, 0, 2, 3).reshape(27, 8, 16, cout)
        gathered = gathered.transpose(1, 0, 2, 3)
    count = lax.dynamic_slice_in_dim(counts, my_grp * num_dev + my_dev, 1)
    parts = terms(count, gathered, x, cot, bias)
    flat = parts[:, :27].transpose(0, 2, 1, 3).reshape(cin * 27, cout)
    part_w = lax.psum_scatter(flat, "dev", scatter_dimension=0, tiled=True)
    part_w = lax.psum(part_w, "grp")
    total_b = lax.psum(parts[0, 27, 0], ("grp", "dev"))
    part_b = lax.dynamic_slice_in_dim(total_b, my_dev * share, share, 0)
    return part_w * scale, part_b * scale


def solution(mesh):
    return jax.shard_map(
        body,
        mesh=mesh,
        in_specs=(
            P(("grp", "dev"), None, None, None, None),
            P(("grp", "dev"), None, None, None, None),
            P("dev", None),
            P(),
            P(),
        ),
        out_specs=(P("dev", None), P("dev")),
        check_vma=False,
    )
```
